512 devices in a mesh: mesh: 32 (over z, core), samp: 16 (over y, x).
Axes of the slice: x: 4, y: 4, z: 16, core: 2. Of those that a mesh axis runs over, the one named last changes fastest.
Arguments:
- resid_in: float32 [1024, 98304], P('samp', 'mesh'), may hold values from -10 to 10
- recycle_u: bfloat16 [64, 98304], P('samp', 'mesh'), may hold values from -0.75 to 0.75
- recycle_c: bfloat16 [64, 98304], P('samp', 'mesh'), may hold values from -0.01953125 to 0.01953125
- stiff: bfloat16 [512, 192, 1152], P('mesh'), may hold values from -0.1875 to 0.1875
- diag_scale: float32 [98304], P('mesh'), may hold values from 1 to 8
- pattern: int32 [512, 6], P('mesh'), may hold values from 0 to 31, as said below
- send_list: int32 [64, 8], P('mesh'), may hold values from 0 to 15, as said below
- part_sizes: int32 [32], P('mesh'), may hold values from 8 to 16, as said below
Outputs:
- solution: float32 [1024, 98304], P('samp', 'mesh')
- residual: float32 [1024, 98304], P('samp', 'mesh')
- recycle_coef: float32 [64, 1024], P(None, 'samp')
The draws below stay inside these ranges and needn't reach their ends.
Inputs may be any that keep to these rules, and one draw needn't show every extreme that they name: `part_sizes`: one partition has 16 live blocks and one has 8. Entries of send_list for partition p are live local blocks of p (below part_sizes[p]); repeats may occur. `pattern`: slot 0 of each block row is its own block; entries below 16 name live local blocks, 16 to 23 left ghosts, the rest right ghosts.
All inputs are finite; a program needn't handle non-finite values.
Results may differ from the reference program's by a relative error of at most 0.0063.
Values may be sent and summed in bfloat16 or wider, within the bound.
A program may use at most 64 MiB of HBM per device.

```python
import math
import jax
import jax.numpy as jnp
from jax import lax

BLK = 192
BPP = 16
NNZB = 6
RECY = 64
ITERS = 2
GHOST = 8
NBLK = 512
NDOF = 98304
LOADS = 1024
N_MESH = 32


def draw_live(key):
    partitions = NBLK // BPP
    base = jax.random.fold_in(key, 11)
    keys = jax.random.split(base, 3)
    counts = jax.random.randint(keys[0], (partitions,), BPP // 2, BPP + 1)
    full_at = jax.random.randint(keys[1], (), 0, partitions)
    least_at = (full_at + 1 + jax.random.randint(keys[2], (), 0, partitions - 1)) % partitions
    positions = jnp.arange(partitions)
    counts = jnp.where(positions == full_at, BPP, counts)
    counts = jnp.where(positions == least_at, BPP // 2, counts)
    return counts.astype(jnp.int32)


def draw_part_sizes(key, part):
    return draw_live(key)


def draw_send_list(key, part):
    partitions = NBLK // BPP
    counts = draw_live(key)
    picks = jax.random.randint(jax.random.fold_in(key, 23), (partitions, 2, GHOST), 0, counts[:, None, None])
    picks = picks.at[:, 0, 0].set(counts - 1)
    picks = picks.at[:, 1, 0].set(0)
    return picks.reshape(partitions * 2, GHOST).astype(jnp.int32)


def draw_pattern(key, part):
    partitions = NBLK // BPP
    counts = draw_live(key)[:, None, None]
    raw_cols = jax.random.randint(jax.random.fold_in(key, 37), (partitions, BPP, NNZB - 1), 0, counts + 2 * GHOST)
    ghosted = jnp.where(raw_cols < counts, raw_cols, raw_cols - counts + BPP)
    block_ids = jnp.arange(BPP, dtype=jnp.int32)
    own_cols = jnp.broadcast_to(block_ids[None, :, None], (partitions, BPP, 1))
    table = jnp.concatenate([own_cols, ghosted.astype(jnp.int32)], 2)
    table = table.at[:, 0, 1].set(BPP)
    table = table.at[:, 0, NNZB - 1].set(BPP + 2 * GHOST - 1)
    return table.reshape(NBLK, NNZB).astype(jnp.int32)


def draw_resid_in(key, part):
    ramp = 0.5 + 1.5 * jnp.arange(NDOF, dtype=jnp.float32) / NDOF
    values = jnp.clip(jax.random.normal(key, (LOADS, NDOF), jnp.float32), -5.0, 5.0) * ramp
    return values.astype(jnp.float32)


def shard_levels(own_key, dims, shards, low, top_value):
    loudness, own = 1.0, jax.random.fold_in(own_key, 6)
    for position, shards_of in shards:
        steps = jnp.exp(jax.random.uniform(jax.random.fold_in(own, position), (shards_of,), jnp.float32, low / len(shards), top_value / len(shards)))
        loudness = loudness * jnp.repeat(steps, dims[position] // shards_of).reshape([-1 if axis == position else 1 for axis in range(len(dims))])
    return loudness


def bell_draw(stream_key, extent, scale, most, cuts=(), held_as=jnp.bfloat16):
    result = scale * jax.random.normal(stream_key, extent, jnp.float32)
    if cuts:
        result = result * shard_levels(stream_key, extent, cuts, -0.22, 0.18)
    return jnp.clip(result, -most, most).astype(held_as)


def setup_inputs(seed: int = 0) -> dict:
    arg_keys = jax.random.split(jax.random.key(seed), 9)
    resid_in = draw_resid_in(jax.random.fold_in(arg_keys[8], 71), 0)
    recycle_u = bell_draw(arg_keys[1], (RECY, NDOF), RECY ** -0.5, 0.75, ((0, 16), (1, 32)))
    recycle_c = bell_draw(arg_keys[2], (RECY, NDOF), NDOF ** -0.5, 0.01953125, ((0, 16), (1, 32)))
    stiff = bell_draw(arg_keys[3], (NBLK, BLK, NNZB * BLK), (BLK * NNZB) ** -0.5, 0.1875, ((0, 32),))
    diag_scale = jnp.clip(jnp.exp(math.log(8.0) - 2.0794415 * jax.random.uniform(arg_keys[4], (NDOF,), jnp.float32) ** shard_levels(arg_keys[4], (NDOF,), ((0, 32),), -0.2, 0.2)), 1.0, 8.0)
    pattern = draw_pattern(jax.random.fold_in(arg_keys[8], 71), 0)
    send_list = draw_send_list(jax.random.fold_in(arg_keys[8], 71), 0)
    part_sizes = draw_part_sizes(jax.random.fold_in(arg_keys[8], 71), 0)
    return dict(resid_in=resid_in, recycle_u=recycle_u, recycle_c=recycle_c, stiff=stiff, diag_scale=diag_scale, pattern=pattern, send_list=send_list, part_sizes=part_sizes)


highest = lax.Precision.HIGHEST


def live_mask(part_sizes):
    block_ids = jnp.arange(BPP, dtype=jnp.int32)
    alive_blocks = (block_ids[None, :] < part_sizes[:, None]).astype(jnp.float32)
    return jnp.broadcast_to(alive_blocks[:, :, None], (N_MESH, BPP, BLK)).reshape(NDOF)


def apply_stiff(rounded, stiff, diag_scale, pattern, send_list, alive_mask):
    clusters = rounded.reshape(LOADS, N_MESH, BPP, BLK).transpose(1, 0, 2, 3)
    sends = send_list.reshape(N_MESH, 2, GHOST)
    to_right = jax.vmap(lambda values, chosen: values[:, chosen])(clusters, sends[:, 0])
    to_left = jax.vmap(lambda values, chosen: values[:, chosen])(clusters, sends[:, 1])
    no_ghost = jnp.zeros_like(to_right[:1])
    left_ghost = jnp.concatenate([no_ghost, to_right[:-1]], 0)
    right_ghost = jnp.concatenate([to_left[1:], no_ghost], 0)
    extended = jnp.concatenate([clusters, left_ghost, right_ghost], 2)
    block_vals = stiff.reshape(N_MESH, BPP, BLK, NNZB * BLK)
    columns = pattern.reshape(N_MESH, BPP, NNZB)

    def one_part(member):
        ext_part, vals_part, cols_part = member
        picked = ext_part[:, cols_part].astype(jnp.float32)
        picked = picked.reshape(LOADS, BPP, NNZB * BLK)
        return jnp.einsum("lik,ick->lic", picked, vals_part.astype(jnp.float32), precision=highest)

    coupled = lax.map(one_part, (extended, block_vals, columns))
    coupled = coupled.transpose(1, 0, 2, 3).reshape(LOADS, NDOF)
    return alive_mask * (diag_scale * rounded.astype(jnp.float32) + coupled)


def reference(resid_in, recycle_u, recycle_c, stiff, diag_scale, pattern, send_list, part_sizes):
    alive_mask = live_mask(part_sizes)
    panel_c = recycle_c.astype(jnp.float32)
    panel_u = recycle_u.astype(jnp.float32)
    current = alive_mask * resid_in
    recycle_coef = jnp.dot(recycle_c, current.astype(jnp.bfloat16).T, preferred_element_type=jnp.float32)
    current = current - alive_mask * jnp.dot(recycle_coef.T, panel_c, precision=highest)
    carried = recycle_coef
    direct = jnp.zeros_like(current)
    for iteration in range(ITERS):
        rounded = current.astype(jnp.bfloat16)
        image_vec = apply_stiff(rounded, stiff, diag_scale, pattern, send_list, alive_mask)
        projected = jnp.dot(panel_c, image_vec.T, precision=highest)
        image_vec = image_vec - alive_mask * jnp.dot(projected.T, panel_c, precision=highest)
        step_size = jnp.sum(image_vec * current, axis=1) / jnp.sum(image_vec * image_vec, axis=1)
        direct = direct + step_size[:, None] * rounded.astype(jnp.float32)
        carried = carried - projected * step_size[None, :]
        current = current - step_size[:, None] * image_vec
    solution = alive_mask * jnp.dot(carried.T, panel_u, precision=highest) + direct
    return solution, current, recycle_coef
```

```python
import functools

import jax
import jax.numpy as jnp
from jax import lax
from jax.experimental import pallas as pl
from jax.experimental.pallas import tpu as pltpu
from jax.sharding import PartitionSpec as P

MESH = pl.DeviceIdType.MESH
F32 = jnp.float32
BF16 = jnp.bfloat16
LANES = 128
BLK = 192
PAIR = 2 * BLK
SLOTS = 6
GHOST = 8
ITERS = 2
TILES = 8


def nt(a, b):
    return lax.dot_general(a, b, (((1,), (1,)), ((), ())), preferred_element_type=F32)


def nn(a, b):
    return lax.dot_general(a, b, (((1,), (0,)), ((), ())), preferred_element_type=F32)


def split2(x):
    high = x.astype(BF16)
    low = (x - high.astype(F32)).astype(BF16)
    return jnp.concatenate([high, low], 0)


def halves(x):
    rows = x.shape[0] // 2
    return x[:rows] + x[rows:]


def turned(x):
    return pltpu.roll(x, LANES // 2, 1)


def kernel(
    n_mesh, n_samp,
    resid, u_in, c_in, stiff, diag, pattern, send_list, sizes,
    sol_out, res_out, coef_out,
    r, uc_loc, st, dg, stage, panel_send, panel_got, spread, cn, un,
    rb, t0, t1, r0t, send_a, send_m, got_a, got_m, w, wb, sol, coef_t,
    pay, rs_got, ar_got,
    in_sems, panel_ssem, panel_rsem, ghost_ssem, ghost_rsem, rs_ssem, rs_rsem, ag_ssem, ag_rsem, out_sems,
):
    me = lax.axis_index("mesh")
    mine = lax.axis_index("samp")
    cols, dofs = r.shape
    recy = cn.shape[0]
    rows_per = recy // n_samp
    quarters = 16 // rows_per
    wide = dofs // quarters // LANES
    pairs = dofs // PAIR
    stride = n_mesh // TILES
    live = sizes[0] * BLK
    low_half = lax.broadcasted_iota(jnp.int32, (cols, LANES), 1) < LANES // 2

    def row_alive(start, width):
        return (lax.broadcasted_iota(jnp.int32, (1, width), 1) + start) < live

    loads = [
        pltpu.make_async_copy(c_in, uc_loc.at[0], in_sems.at[0]),
        pltpu.make_async_copy(u_in, uc_loc.at[1], in_sems.at[1]),
        pltpu.make_async_copy(resid, r, in_sems.at[2]),
        pltpu.make_async_copy(diag, dg, in_sems.at[3]),
        pltpu.make_async_copy(stiff, st, in_sems.at[4]),
    ]
    for load in loads:
        load.start()

    barrier = pltpu.get_barrier_semaphore()

    def greet_mesh(o, carry):
        pl.semaphore_signal(barrier, inc=1, device_id={"mesh": lax.rem(me + o, n_mesh)}, device_id_type=MESH)
        return carry

    def greet_samp(o, carry):
        pl.semaphore_signal(barrier, inc=1, device_id={"samp": lax.rem(mine + o, n_samp)}, device_id_type=MESH)
        return carry

    lax.fori_loop(1, n_samp, greet_samp, 0)
    lax.fori_loop(1, n_mesh, greet_mesh, 0)

    def pack_panel(which):
        local = uc_loc[which].astype(F32)
        for q in range(quarters):
            for t in range(wide):
                at = (q * wide + t) * LANES
                stage[which, t, pl.ds(q, rows_per, stride=quarters), :] = local[:, at : at + LANES]
        packed = stage[which].astype(BF16)
        panel_send[which] = packed
        panel_got[which, mine] = packed

    def send_panel(which):
        def one(o, carry):
            pltpu.make_async_remote_copy(
                src_ref=panel_send.at[which],
                dst_ref=panel_got.at[which, mine],
                send_sem=panel_ssem.at[which],
                recv_sem=panel_rsem.at[which],
                device_id={"samp": lax.rem(mine + o, n_samp)},
                device_id_type=MESH,
            ).start()
            return carry

        lax.fori_loop(1, n_samp, one, 0)

    def wait_panel(which):
        others = panel_got.at[which, pl.ds(0, n_samp - 1)]
        pltpu.make_async_copy(others, others, panel_rsem.at[which]).wait()

    def panel_sent(which):
        others = panel_got.at[which, pl.ds(0, n_samp - 1)]
        pltpu.make_async_copy(others, others, panel_ssem.at[which]).wait()

    def natural(which, out):
        for k in range(n_samp):
            for t in range(wide):
                spread[t, 16 * k : 16 * k + 16, :] = panel_got[which, k, t].astype(F32)
        for q in range(quarters):
            for t in range(wide):
                at = (q * wide + t) * LANES
                tile = spread[t, pl.ds(q, recy, stride=quarters), :]
                out[:, at : at + LANES] = jnp.where(row_alive(at, LANES), tile, 0.0).astype(BF16)

    part = lax.div(me, stride)
    reducer = lax.rem(me, stride) == 0

    def rs_send(which, value):
        for t in range(TILES):
            pay[which, t] = value[8 * t : 8 * t + 8, :]

        @pl.when(reducer)
        def _():
            rs_got[which, me] = pay[which, part]

        def one(o, carry):
            t = lax.rem(part + o, TILES)
            target = t * stride

            @pl.when(target != me)
            def _():
                pltpu.make_async_remote_copy(
                    src_ref=pay.at[which, t],
                    dst_ref=rs_got.at[which, me],
                    send_sem=rs_ssem.at[which],
                    recv_sem=rs_rsem.at[which],
                    device_id={"mesh": target},
                    device_id_type=MESH,
                ).start()

            return carry

        lax.fori_loop(0, TILES, one, 0)

    def ag_send(which):
        @pl.when(reducer)
        def _():
            others = rs_got.at[which, pl.ds(0, n_mesh - 1)]
            pltpu.make_async_copy(others, others, rs_rsem.at[which]).wait()
            total = rs_got[which, 0]
            for d in range(1, n_mesh):
                total = total + rs_got[which, d]
            ar_got[which, part] = total

            def one(o, carry):
                pltpu.make_async_remote_copy(
                    src_ref=ar_got.at[which, part],
                    dst_ref=ar_got.at[which, part],
                    send_sem=ag_ssem.at[which],
                    recv_sem=ag_rsem.at[which],
                    device_id={"mesh": lax.rem(me + o, n_mesh)},
                    device_id_type=MESH,
                ).start()
                return carry

            lax.fori_loop(1, n_mesh, one, 0)

    def ar_wait(which):
        @pl.when(reducer)
        def _():
            some = ar_got.at[which, pl.ds(0, TILES - 1)]
            pltpu.make_async_copy(some, some, ag_rsem.at[which]).wait()

        @pl.when(jnp.logical_not(reducer))
        def _():
            pltpu.make_async_copy(ar_got.at[which], ar_got.at[which], ag_rsem.at[which]).wait()

        return jnp.concatenate([ar_got[which, t] for t in range(TILES)], 0)

    def ar_sent(which):
        @pl.when(reducer)
        def _():
            some = ar_got.at[which, pl.ds(0, TILES - 1)]
            pltpu.make_async_copy(some, some, rs_ssem.at[which]).wait()
            others = rs_got.at[which, pl.ds(0, n_mesh - 1)]
            pltpu.make_async_copy(others, others, ag_ssem.at[which]).wait()

        @pl.when(jnp.logical_not(reducer))
        def _():
            pltpu.make_async_copy(ar_got.at[which], ar_got.at[which], rs_ssem.at[which]).wait()

    def fill_tables(m, n0, n1, n2):
        b0, b1, b2 = n0.astype(BF16), n1.astype(BF16), n2.astype(BF16)
        v0, v1, v2 = turned(n0).astype(BF16), turned(n1).astype(BF16), turned(n2).astype(BF16)
        even, odd = 2 * m, 2 * m + 1
        t0[even] = b0
        r0t[even] = v0
        t1[even] = jnp.where(low_half, b1, v1)
        t0[odd] = jnp.where(low_half, v1, v2)
        r0t[odd] = jnp.where(low_half, b2, b1)
        t1[odd] = jnp.where(low_half, v2, b2)

    def ghost_copies(it):
        out = []
        for side, by in ((0, 1), (1, n_mesh - 1)):
            peer = {"mesh": lax.rem(me + by, n_mesh)}
            for j, (src, dst) in enumerate(((send_a, got_a), (send_m, got_m))):
                out.append(
                    pltpu.make_async_remote_copy(
                        src_ref=src.at[it, side],
                        dst_ref=dst.at[it, side],
                        send_sem=ghost_ssem.at[it, side, j],
                        recv_sem=ghost_rsem.at[it, side, j],
                        device_id=peer,
                        device_id_type=MESH,
                    )
                )
        return out

    def send_ghosts(it):
        ends = (me == n_mesh - 1, me == 0)
        for side in range(2):
            keep = jnp.where(ends[side], 0.0, 1.0).astype(BF16)
            for pair in range(GHOST // 2):
                a, b = send_list[side, 2 * pair], send_list[side, 2 * pair + 1]
                send_a[it, side, 2 * pair] = t0[a] * keep
                send_a[it, side, 2 * pair + 1] = t0[b] * keep
                send_m[it, side, pair] = jnp.where(low_half, t1[a], t1[b]) * keep
        copies = ghost_copies(it)
        for copy in copies:
            copy.start()

    def take_ghosts(it):
        for copy in ghost_copies(it):
            copy.wait()
        for side in range(2):
            base = 2 * pairs + side * GHOST
            for pair in range(GHOST // 2):
                for j in range(2):
                    x = got_a[it, side, 2 * pair + j]
                    t0[base + 2 * pair + j] = x
                    r0t[base + 2 * pair + j] = turned(x.astype(F32)).astype(BF16)
                x = got_m[it, side, pair]
                y = turned(x.astype(F32)).astype(BF16)
                t1[base + 2 * pair] = jnp.where(low_half, x, y)
                t1[base + 2 * pair + 1] = jnp.where(low_half, y, x)

    def gathered(i):
        parts = []
        for s in range(0, SLOTS, 2):
            a, b = pattern[i, s], pattern[i, s + 1]
            turned_b, tail_b = r0t[b], t1[b]
            parts.append(t0[a])
            parts.append(jnp.where(low_half, t1[a], turned_b))
            parts.append(jnp.where(low_half, turned_b, tail_b))
        return jnp.concatenate(parts, 1)

    def apply_stiff(it):
        def pair_step(m, carry):
            ww, wr = carry
            at = pl.multiple_of(m * PAIR, PAIR)
            out0 = nt(gathered(2 * m), st[pl.ds(at, 2 * LANES), :])
            out1 = nt(gathered(2 * m + 1), st[pl.ds(at + LANES, 2 * LANES), :])
            coupled = (
                out0[:, :LANES],
                jnp.where(low_half, out0[:, LANES:], out1[:, :LANES]),
                out1[:, LANES:],
            )
            for j in range(3):
                span = pl.ds(at + j * LANES, LANES)
                rounded = rb[it, :, span].astype(F32)
                image = jnp.where(
                    row_alive(at + j * LANES, LANES), dg[:, span] * rounded + coupled[j], 0.0
                )
                w[:, span] = image
                high = image.astype(BF16)
                wb[:cols, span] = high
                wb[cols:, span] = (image - high.astype(F32)).astype(BF16)
                ww = ww + image * image
                wr = wr + image * r[:, span]
            return ww, wr

        zero = jnp.zeros((cols, LANES), F32)
        ww, wr = lax.fori_loop(0, pairs, pair_step, (zero, zero))
        proj = halves(nt(wb[...], cn[...]))
        ww = jnp.sum(ww, axis=1, keepdims=True)
        wr = jnp.sum(wr, axis=1, keepdims=True)
        lane = lax.broadcasted_iota(jnp.int32, (cols, LANES - recy), 1)
        return jnp.concatenate([proj, jnp.where(lane == 0, ww, jnp.where(lane == 1, wr, 0.0))], 1)

    loads[0].wait()
    pack_panel(0)
    pl.semaphore_wait(barrier, n_mesh + n_samp - 2)
    send_panel(0)
    loads[1].wait()
    pack_panel(1)
    send_panel(1)
    loads[2].wait()
    for m in range(pairs):
        at = m * PAIR
        r[:, at : at + PAIR] = jnp.where(row_alive(at, PAIR), r[:, at : at + PAIR], 0.0)
        rb[0, :, at : at + PAIR] = r[:, at : at + PAIR].astype(BF16)
    wait_panel(0)
    natural(0, cn)
    first = nt(jnp.concatenate([rb[0], cn[...]], 0), cn[...])
    rs_send(0, jnp.concatenate([first[:cols], first[cols:]], 1))
    loads[3].wait()
    wait_panel(1)
    natural(1, un)
    loads[4].wait()
    ag_send(0)
    reduced = ar_wait(0)
    carried = reduced[:, :recy]
    gram = reduced[:, recy:]
    coef_t[...] = carried.T
    coef_copy = pltpu.make_async_copy(coef_t, coef_out, out_sems.at[0])
    coef_copy.start()
    highest = lax.Precision.HIGHEST
    c_r = carried - jnp.dot(carried, gram, precision=highest, preferred_element_type=F32)

    coef2 = split2(carried)

    def first_update(m, carry):
        span = pl.ds(pl.multiple_of(m * PAIR, PAIR), PAIR)
        new = r[:, span] - halves(nn(coef2, cn[:, span]))
        r[:, span] = new
        rb[0, :, span] = new.astype(BF16)
        fill_tables(m, new[:, :LANES], new[:, LANES : 2 * LANES], new[:, 2 * LANES :])
        return carry

    lax.fori_loop(0, pairs, first_update, 0)

    steps = []
    for it in range(ITERS):
        send_ghosts(it)
        take_ghosts(it)
        rs_send(it + 1, apply_stiff(it))
        ag_send(it + 1)
        reduced = ar_wait(it + 1)
        proj = reduced[:, :recy]
        ww = reduced[:, recy : recy + 1]
        wr = reduced[:, recy + 1 : recy + 2]
        p_gram = jnp.dot(proj, gram, precision=highest, preferred_element_type=F32)
        bottom = ww + jnp.sum(proj * (p_gram - 2.0 * proj), axis=1, keepdims=True)
        top = wr - jnp.sum(proj * c_r, axis=1, keepdims=True)
        step = top / bottom
        steps.append(step)
        c_r = c_r - step * (proj - p_gram)
        carried = carried - step * proj
        proj2 = split2(proj)
        if it + 1 < ITERS:

            def update(m, carry):
                span = pl.ds(pl.multiple_of(m * PAIR, PAIR), PAIR)
                new = r[:, span] - step * (w[:, span] - halves(nn(proj2, cn[:, span])))
                r[:, span] = new
                rb[it + 1, :, span] = new.astype(BF16)
                fill_tables(m, new[:, :LANES], new[:, LANES : 2 * LANES], new[:, 2 * LANES :])
                return carry

            lax.fori_loop(0, pairs, update, 0)
        else:
            carried2 = split2(carried)

            def finish(m, carry):
                span = pl.ds(pl.multiple_of(m * PAIR, PAIR), PAIR)
                r[:, span] = r[:, span] - step * (w[:, span] - halves(nn(proj2, cn[:, span])))
                direct = steps[0] * rb[0, :, span].astype(F32)
                for j in range(1, ITERS):
                    direct = direct + steps[j] * rb[j, :, span].astype(F32)
                sol[:, span] = halves(nn(carried2, un[:, span])) + direct
                return carry

            lax.fori_loop(0, pairs, finish, 0)

    outs = [
        coef_copy,
        pltpu.make_async_copy(r, res_out, out_sems.at[1]),
        pltpu.make_async_copy(sol, sol_out, out_sems.at[2]),
    ]
    for copy in outs[1:]:
        copy.start()
    for which in range(ITERS + 1):
        ar_sent(which)
    for which in range(2):
        panel_sent(which)
    for copy in outs:
        copy.wait()


def per_device(resid_in, recycle_u, recycle_c, stiff, diag_scale, pattern, send_list, part_sizes, n_mesh, n_samp):
    cols, dofs = resid_in.shape
    blocks, blk, width = stiff.shape
    recy = recycle_c.shape[0] * n_samp
    wide = dofs * recycle_c.shape[0] // 16 // LANES
    ext = blocks + 2 * GHOST
    hbm = pl.BlockSpec(memory_space=pl.ANY)
    smem = pl.BlockSpec(memory_space=pltpu.SMEM)
    dma = pltpu.SemaphoreType.DMA
    return pl.pallas_call(
        functools.partial(kernel, n_mesh, n_samp),
        out_shape=(
            jax.ShapeDtypeStruct((cols, dofs), F32),
            jax.ShapeDtypeStruct((cols, dofs), F32),
            jax.ShapeDtypeStruct((recy, cols), F32),
        ),
        in_specs=[hbm, hbm, hbm, hbm, hbm, smem, smem, smem],
        out_specs=(hbm, hbm, hbm),
        scratch_shapes=[
            pltpu.VMEM((cols, dofs), F32),
            pltpu.VMEM((2, recycle_c.shape[0], dofs), BF16),
            pltpu.VMEM((blocks * blk, width), BF16),
            pltpu.VMEM((1, dofs), F32),
            pltpu.VMEM((2, wide, 16, LANES), F32),
            pltpu.VMEM((2, wide, 16, LANES), BF16),
            pltpu.VMEM((2, n_samp, wide, 16, LANES), BF16),
            pltpu.VMEM((wide, 16 * n_samp, LANES), F32),
            pltpu.VMEM((recy, dofs), BF16),
            pltpu.VMEM((recy, dofs), BF16),
            pltpu.VMEM((ITERS, cols, dofs), BF16),
            pltpu.VMEM((ext, cols, LANES), BF16),
            pltpu.VMEM((ext, cols, LANES), BF16),
            pltpu.VMEM((ext, cols, LANES), BF16),
            pltpu.VMEM((ITERS, 2, GHOST, cols, LANES), BF16),
            pltpu.VMEM((ITERS, 2, GHOST // 2, cols, LANES), BF16),
            pltpu.VMEM((ITERS, 2, GHOST, cols, LANES), BF16),
            pltpu.VMEM((ITERS, 2, GHOST // 2, cols, LANES), BF16),
            pltpu.VMEM((cols, dofs), F32),
            pltpu.VMEM((2 * cols, dofs), BF16),
            pltpu.VMEM((cols, dofs), F32),
            pltpu.VMEM((recy, cols), F32),
            pltpu.VMEM((ITERS + 1, TILES, 8, LANES), F32),
            pltpu.VMEM((ITERS + 1, n_mesh, 8, LANES), F32),
            pltpu.VMEM((ITERS + 1, TILES, 8, LANES), F32),
            dma((5,)),
            dma((2,)),
            dma((2,)),
            dma((ITERS, 2, 2)),
            dma((ITERS, 2, 2)),
            dma((ITERS + 1,)),
            dma((ITERS + 1,)),
            dma((ITERS + 1,)),
            dma((ITERS + 1,)),
            dma((3,)),
        ],
        compiler_params=pltpu.CompilerParams(
            collective_id=0, has_side_effects=True, vmem_limit_bytes=48 << 20
        ),
    )(
        resid_in,
        recycle_u,
        recycle_c,
        stiff.reshape(blocks * blk, width),
        diag_scale.reshape(1, dofs),
        pattern,
        send_list,
        part_sizes,
    )


def solution(mesh):
    body = functools.partial(per_device, n_mesh=mesh.shape["mesh"], n_samp=mesh.shape["samp"])
    return jax.shard_map(
        body,
        mesh=mesh,
        in_specs=(
            P("samp", "mesh"),
            P("samp", "mesh"),
            P("samp", "mesh"),
            P("mesh", None, None),
            P("mesh"),
            P("mesh", None),
            P("mesh", None),
            P("mesh"),
        ),
        out_specs=(P("samp", "mesh"), P("samp", "mesh"), P(None, "samp")),
        check_vma=False,
    )
```

```python
import functools

import jax
import jax.numpy as jnp
from jax import lax
from jax.experimental import pallas as pl
from jax.experimental.pallas import tpu as pltpu
from jax.sharding import PartitionSpec as P

MESH = pl.DeviceIdType.MESH
F32 = jnp.float32
BF16 = jnp.bfloat16
LANES = 128
BLK = 192
PAIR = 2 * BLK
SLOTS = 6
GHOST = 8
ITERS = 2
TILES = 8


def nt(a, b):
    return lax.dot_general(a, b, (((1,), (1,)), ((), ())), preferred_element_type=F32)


def nn(a, b):
    return lax.dot_general(a, b, (((1,), (0,)), ((), ())), preferred_element_type=F32)


def split2(x):
    high = x.astype(BF16)
    low = (x - high.astype(F32)).astype(BF16)
    return jnp.concatenate([high, low], 0)


def halves(x):
    rows = x.shape[0] // 2
    return x[:rows] + x[rows:]


def turned(x):
    return pltpu.roll(x, LANES // 2, 1)


def kernel(
    n_mesh, n_samp,
    resid, u_in, c_in, stiff, diag, pattern_in, send_in, sizes_in,
    sol_out, res_out, coef_out,
    r, a, b, r_next, w_next, sol, coef_t,
    uc_loc, st, dg, pattern, send_list, sizes,
    stage, panel_send, panel_got, spread, cn, un, dn, rb, wb,
    t0, t1, r0t, send_f, got_f, send_c, got_c,
    pay, rs_got, ar_got,
    in_sems, panel_ssem, panel_rsem, ghost_ssem, ghost_rsem, rs_ssem, rs_rsem, ag_ssem, ag_rsem, out_sems,
):
    me = lax.axis_index("mesh")
    mine = lax.axis_index("samp")
    cols, dofs = r.shape
    recy = cn.shape[0]
    rows_per = recy // n_samp
    quarters = 16 // rows_per
    wide = dofs // quarters // LANES
    pairs = dofs // PAIR
    stride = n_mesh // TILES
    low_half = lax.broadcasted_iota(jnp.int32, (cols, LANES), 1) < LANES // 2
    highest = lax.Precision.HIGHEST

    loads = [
        pltpu.make_async_copy(src, dst, in_sems.at[i])
        for i, (src, dst) in enumerate(
            (
                (c_in, uc_loc.at[0]),
                (sizes_in, sizes),
                (resid, r),
                (send_in, send_list),
                (u_in, uc_loc.at[1]),
                (diag, dg),
                (pattern_in, pattern),
                (stiff, st),
            )
        )
    ]
    for load in loads:
        load.start()

    barrier = pltpu.get_barrier_semaphore()

    def greet_mesh(o, carry):
        pl.semaphore_signal(barrier, inc=1, device_id={"mesh": lax.rem(me + o, n_mesh)}, device_id_type=MESH)
        return carry

    def greet_samp(o, carry):
        pl.semaphore_signal(barrier, inc=1, device_id={"samp": lax.rem(mine + o, n_samp)}, device_id_type=MESH)
        return carry

    lax.fori_loop(1, n_mesh, greet_mesh, 0)
    lax.fori_loop(1, n_samp, greet_samp, 0)

    def row_alive(start, width):
        live = sizes[0] * BLK
        return (lax.broadcasted_iota(jnp.int32, (1, width), 1) + start) < live

    def pack_panel(which):
        local = uc_loc[which].astype(F32)
        for q in range(quarters):
            for t in range(wide):
                at = (q * wide + t) * LANES
                stage[which, t, pl.ds(q, rows_per, stride=quarters), :] = local[:, at : at + LANES]
        packed = stage[which].astype(BF16)
        panel_send[which] = packed
        panel_got[which, mine] = packed

    def send_panel(which):
        def one(o, carry):
            pltpu.make_async_remote_copy(
                src_ref=panel_send.at[which],
                dst_ref=panel_got.at[which, mine],
                send_sem=panel_ssem.at[which],
                recv_sem=panel_rsem.at[which],
                device_id={"samp": lax.rem(mine + o, n_samp)},
                device_id_type=MESH,
            ).start()
            return carry

        lax.fori_loop(1, n_samp, one, 0)

    def wait_panel(which, sems):
        others = panel_got.at[which, pl.ds(0, n_samp - 1)]
        pltpu.make_async_copy(others, others, sems.at[which]).wait()

    def natural(which, out):
        for k in range(n_samp):
            for t in range(wide):
                spread[t, 16 * k : 16 * k + 16, :] = panel_got[which, k, t].astype(F32)
        for q in range(quarters):
            for t in range(wide):
                at = (q * wide + t) * LANES
                tile = spread[t, pl.ds(q, recy, stride=quarters), :]
                out[:, at : at + LANES] = jnp.where(row_alive(at, LANES), tile, 0.0).astype(BF16)

    part = lax.div(me, stride)
    reducer = lax.rem(me, stride) == 0

    def rs_send(which, value):
        for t in range(TILES):
            pay[which, t] = value[8 * t : 8 * t + 8, :]

        @pl.when(reducer)
        def _():
            rs_got[which, me] = pay[which, part]

        def one(o, carry):
            t = lax.rem(part + o, TILES)
            target = t * stride

            @pl.when(target != me)
            def _():
                pltpu.make_async_remote_copy(
                    src_ref=pay.at[which, t],
                    dst_ref=rs_got.at[which, me],
                    send_sem=rs_ssem.at[which],
                    recv_sem=rs_rsem.at[which],
                    device_id={"mesh": target},
                    device_id_type=MESH,
                ).start()

            return carry

        lax.fori_loop(0, TILES, one, 0)

    def ag_send(which):
        @pl.when(reducer)
        def _():
            others = rs_got.at[which, pl.ds(0, n_mesh - 1)]
            pltpu.make_async_copy(others, others, rs_rsem.at[which]).wait()
            total = rs_got[which, 0]
            for d in range(1, n_mesh):
                total = total + rs_got[which, d]
            ar_got[which, part] = total

            def one(o, carry):
                pltpu.make_async_remote_copy(
                    src_ref=ar_got.at[which, part],
                    dst_ref=ar_got.at[which, part],
                    send_sem=ag_ssem.at[which],
                    recv_sem=ag_rsem.at[which],
                    device_id={"mesh": lax.rem(me + o, n_mesh)},
                    device_id_type=MESH,
                ).start()
                return carry

            lax.fori_loop(1, n_mesh, one, 0)

    def ar_wait(which):
        @pl.when(reducer)
        def _():
            some = ar_got.at[which, pl.ds(0, TILES - 1)]
            pltpu.make_async_copy(some, some, ag_rsem.at[which]).wait()

        @pl.when(jnp.logical_not(reducer))
        def _():
            pltpu.make_async_copy(ar_got.at[which], ar_got.at[which], ag_rsem.at[which]).wait()

        return jnp.concatenate([ar_got[which, t] for t in range(TILES)], 0)

    def ar_sent(which):
        @pl.when(reducer)
        def _():
            some = ar_got.at[which, pl.ds(0, TILES - 1)]
            pltpu.make_async_copy(some, some, rs_ssem.at[which]).wait()
            others = rs_got.at[which, pl.ds(0, n_mesh - 1)]
            pltpu.make_async_copy(others, others, ag_ssem.at[which]).wait()

        @pl.when(jnp.logical_not(reducer))
        def _():
            pltpu.make_async_copy(ar_got.at[which], ar_got.at[which], rs_ssem.at[which]).wait()

    def fill_tables(m, row, tiles):
        n0, n1, n2 = tiles
        b0, b1, b2 = n0.astype(BF16), n1.astype(BF16), n2.astype(BF16)
        v0, v1, v2 = turned(n0).astype(BF16), turned(n1).astype(BF16), turned(n2).astype(BF16)
        even, odd, rows = 2 * m, 2 * m + 1, slice(row, row + cols)
        t0[even, rows] = b0
        r0t[even, rows] = v0
        t1[even, rows] = jnp.where(low_half, b1, v1)
        t0[odd, rows] = jnp.where(low_half, v1, v2)
        r0t[odd, rows] = jnp.where(low_half, b2, b1)
        t1[odd, rows] = jnp.where(low_half, v2, b2)

    def fill_split(source):
        def one(m, carry):
            at = pl.multiple_of(m * PAIR, PAIR)
            tiles = [source[:, pl.ds(at + j * LANES, LANES)] for j in range(3)]
            fill_tables(m, 0, tiles)
            fill_tables(m, cols, [x - x.astype(BF16).astype(F32) for x in tiles])
            return carry

        lax.fori_loop(0, pairs, one, 0)

    def ghost_copies(send, got, which):
        out = []
        for side, by in ((0, 1), (1, n_mesh - 1)):
            out.append(
                pltpu.make_async_remote_copy(
                    src_ref=send.at[side],
                    dst_ref=got.at[side],
                    send_sem=ghost_ssem.at[which, side],
                    recv_sem=ghost_rsem.at[which, side],
                    device_id={"mesh": lax.rem(me + by, n_mesh)},
                    device_id_type=MESH,
                )
            )
        return out

    def pack_ghosts(send, row, rows):
        ends = (me == n_mesh - 1, me == 0)
        for side in range(2):
            keep = jnp.where(ends[side], 0.0, 1.0).astype(BF16)
            for start in range(0, rows, cols):
                span, to = slice(row + start, row + start + cols), slice(start, start + cols)
                for pair in range(GHOST // 2):
                    x, y = send_list[side, 2 * pair], send_list[side, 2 * pair + 1]
                    send[side, 2 * pair, to] = t0[x, span] * keep
                    send[side, 2 * pair + 1, to] = t0[y, span] * keep
                    send[side, GHOST + pair, to] = jnp.where(low_half, t1[x, span], t1[y, span]) * keep

    def take_ghosts(got, row, rows):
        for side in range(2):
            base = 2 * pairs + side * GHOST
            for start in range(0, rows, cols):
                span, to = slice(start, start + cols), slice(row + start, row + start + cols)
                for pair in range(GHOST // 2):
                    for j in range(2):
                        x = got[side, 2 * pair + j, span]
                        t0[base + 2 * pair + j, to] = x
                        r0t[base + 2 * pair + j, to] = turned(x.astype(F32)).astype(BF16)
                    x = got[side, GHOST + pair, span]
                    y = turned(x.astype(F32)).astype(BF16)
                    t1[base + 2 * pair, to] = jnp.where(low_half, x, y)
                    t1[base + 2 * pair + 1, to] = jnp.where(low_half, y, x)

    def apply_stiff(rows, emit):
        low_rows = lax.broadcasted_iota(jnp.int32, (rows, LANES), 1) < LANES // 2

        def gathered(i):
            parts = []
            for s in range(0, SLOTS, 2):
                x, y = pattern[i, s], pattern[i, s + 1]
                turned_y = r0t[y, :rows]
                parts.append(t0[x, :rows])
                parts.append(jnp.where(low_rows, t1[x, :rows], turned_y))
                parts.append(jnp.where(low_rows, turned_y, t1[y, :rows]))
            return jnp.concatenate(parts, 1)

        def one(m, carry):
            at = pl.multiple_of(m * PAIR, PAIR)
            out0 = nt(gathered(2 * m), st[pl.ds(at, 2 * LANES), :])
            out1 = nt(gathered(2 * m + 1), st[pl.ds(at + LANES, 2 * LANES), :])
            emit(at, 0, out0[:, :LANES])
            emit(at, 1, jnp.where(low_rows, out0[:, LANES:], out1[:, :LANES]))
            emit(at, 2, out1[:, LANES:])
            return carry

        lax.fori_loop(0, pairs, one, 0)

    def emit_first(at, j, value):
        span = pl.ds(at + j * LANES, LANES)
        keep, scale = row_alive(at + j * LANES, LANES), dg[:, span]
        a[:, span] = jnp.where(keep, halves(value[: 2 * cols]) + scale * r[:, span], 0.0)
        dn[:, span] = jnp.where(keep, value[2 * cols :] + scale * cn[:, span].astype(F32), 0.0).astype(BF16)

    def emit_second(at, j, value):
        span = pl.ds(at + j * LANES, LANES)
        b[:, span] = jnp.where(
            row_alive(at + j * LANES, LANES), halves(value) + dg[:, span] * a[:, span], 0.0
        )

    def renew(make, r_to, w_to):
        def one(m, carry):
            ww, wr = carry
            at = pl.multiple_of(m * PAIR, PAIR)
            span = pl.ds(at, PAIR)
            new_r, image = make(span)
            r_to[:, span] = new_r
            w_to[:, span] = image
            high = image.astype(BF16)
            wb[:cols, span] = high
            wb[cols:, span] = (image - high.astype(F32)).astype(BF16)
            for j in range(3):
                x = image[:, j * LANES : (j + 1) * LANES]
                ww = ww + x * x
                wr = wr + x * new_r[:, j * LANES : (j + 1) * LANES]
            return ww, wr

        zero = jnp.zeros((cols, LANES), F32)
        ww, wr = lax.fori_loop(0, pairs, one, (zero, zero))
        proj = halves(nt(wb[...], cn[...]))
        ww = jnp.sum(ww, axis=1, keepdims=True)
        wr = jnp.sum(wr, axis=1, keepdims=True)
        lane = lax.broadcasted_iota(jnp.int32, (cols, LANES - recy), 1)
        return jnp.concatenate([proj, jnp.where(lane == 0, ww, jnp.where(lane == 1, wr, 0.0))], 1)

    def step_of(reduced, c_r):
        proj = reduced[:, :recy]
        ww = reduced[:, recy : recy + 1]
        wr = reduced[:, recy + 1 : recy + 2]
        p_gram = jnp.dot(proj, gram, precision=highest, preferred_element_type=F32)
        bottom = ww + jnp.sum(proj * (p_gram - 2.0 * proj), axis=1, keepdims=True)
        top = wr - jnp.sum(proj * c_r, axis=1, keepdims=True)
        step = top / bottom
        return proj, step, c_r - step * (proj - p_gram)

    loads[0].wait()
    pack_panel(0)
    loads[1].wait()
    loads[2].wait()

    def mask(m, carry):
        at = pl.multiple_of(m * PAIR, PAIR)
        span = pl.ds(at, PAIR)
        kept = jnp.where(row_alive(at, PAIR), r[:, span], 0.0)
        r[:, span] = kept
        rb[:, span] = kept.astype(BF16)
        return carry

    lax.fori_loop(0, pairs, mask, 0)
    fill_split(r)
    loads[3].wait()
    pack_ghosts(send_f.at[0], 0, 2 * cols)
    loads[4].wait()
    pack_panel(1)
    pl.semaphore_wait(barrier, n_mesh + n_samp - 2)
    send_panel(0)
    for copy in ghost_copies(send_f.at[0], got_f.at[0], 0):
        copy.start()
    send_panel(1)
    wait_panel(0, panel_rsem)
    natural(0, cn)
    first = nt(jnp.concatenate([rb[...], cn[...]], 0), cn[...])
    rs_send(0, jnp.concatenate([first[:cols], first[cols:]], 1))

    def fill_panel(m, carry):
        at = pl.multiple_of(m * PAIR, PAIR)
        fill_tables(m, 2 * cols, [cn[:, pl.ds(at + j * LANES, LANES)].astype(F32) for j in range(3)])
        return carry

    lax.fori_loop(0, pairs, fill_panel, 0)
    pack_ghosts(send_c, 2 * cols, recy)
    for copy in ghost_copies(send_c, got_c, 1):
        copy.start()
    for copy in ghost_copies(send_f.at[0], got_f.at[0], 0):
        copy.wait()
    take_ghosts(got_f.at[0], 0, 2 * cols)
    wait_panel(1, panel_rsem)
    natural(1, un)
    for load in loads[5:]:
        load.wait()
    for copy in ghost_copies(send_c, got_c, 1):
        copy.wait()
    take_ghosts(got_c, 2 * cols, recy)
    ag_send(0)
    apply_stiff(2 * cols + recy, emit_first)
    reduced = ar_wait(0)
    coef = reduced[:, :recy]
    gram = reduced[:, recy:]
    coef2 = split2(coef)

    def make_first(span):
        new_r = r[:, span] - halves(nn(coef2, cn[:, span]))
        return new_r, a[:, span] - halves(nn(coef2, dn[:, span]))

    rs_send(1, renew(make_first, r, a))

    coef_t[...] = coef.T
    coef_copy = pltpu.make_async_copy(coef_t, coef_out, out_sems.at[0])
    coef_copy.start()
    c_r = coef - jnp.dot(coef, gram, precision=highest, preferred_element_type=F32)
    fill_split(a)
    pack_ghosts(send_f.at[1], 0, 2 * cols)
    for copy in ghost_copies(send_f.at[1], got_f.at[1], 2):
        copy.start()
    for copy in ghost_copies(send_f.at[1], got_f.at[1], 2):
        copy.wait()
    take_ghosts(got_f.at[1], 0, 2 * cols)
    ag_send(1)
    apply_stiff(2 * cols, emit_second)
    proj, step1, c_r = step_of(ar_wait(1), c_r)
    proj2 = split2(proj)

    def make_second(span):
        image = a[:, span]
        new_r = r[:, span] - step1 * (image - halves(nn(proj2, cn[:, span])))
        return new_r, image - step1 * (b[:, span] - halves(nn(proj2, dn[:, span])))

    rs_send(2, renew(make_second, r_next, w_next))

    carried2 = split2(coef - step1 * proj)

    def base(m, carry):
        span = pl.ds(pl.multiple_of(m * PAIR, PAIR), PAIR)
        rounded = r[:, span].astype(BF16).astype(F32)
        sol[:, span] = halves(nn(carried2, un[:, span])) + step1 * rounded
        return carry

    lax.fori_loop(0, pairs, base, 0)
    ag_send(2)
    proj, step2, _ = step_of(ar_wait(2), c_r)
    proj2 = split2(proj)

    def finish(m, carry):
        span = pl.ds(pl.multiple_of(m * PAIR, PAIR), PAIR)
        old = r_next[:, span]
        r[:, span] = old - step2 * (w_next[:, span] - halves(nn(proj2, cn[:, span])))
        rounded = old.astype(BF16).astype(F32)
        sol[:, span] = sol[:, span] + step2 * (rounded - halves(nn(proj2, un[:, span])))
        return carry

    lax.fori_loop(0, pairs, finish, 0)
    outs = [
        coef_copy,
        pltpu.make_async_copy(r, res_out, out_sems.at[1]),
        pltpu.make_async_copy(sol, sol_out, out_sems.at[2]),
    ]
    for copy in outs[1:]:
        copy.start()
    for which in range(ITERS + 1):
        ar_sent(which)
    for which in range(2):
        wait_panel(which, panel_ssem)
    for copy in outs:
        copy.wait()


def per_device(resid_in, recycle_u, recycle_c, stiff, diag_scale, pattern, send_list, part_sizes, n_mesh, n_samp):
    cols, dofs = resid_in.shape
    blocks, blk, width = stiff.shape
    recy = recycle_c.shape[0] * n_samp
    wide = dofs * recycle_c.shape[0] // 16 // LANES
    ext = blocks + 2 * GHOST
    hbm = pl.BlockSpec(memory_space=pltpu.HBM)
    dma = pltpu.SemaphoreType.DMA
    field = pltpu.VMEM((cols, dofs), F32)
    panel = pltpu.VMEM((recy, dofs), BF16)
    table = pltpu.VMEM((ext, 2 * cols + recy, LANES), BF16)
    return pl.pallas_call(
        functools.partial(kernel, n_mesh, n_samp),
        out_shape=(
            jax.ShapeDtypeStruct((cols, dofs), F32),
            jax.ShapeDtypeStruct((cols, dofs), F32),
            jax.ShapeDtypeStruct((recy, cols), F32),
        ),
        in_specs=[hbm] * 8,
        out_specs=(hbm, hbm, hbm),
        scratch_shapes=[
            field,
            field,
            field,
            field,
            field,
            field,
            pltpu.VMEM((recy, cols), F32),
            pltpu.VMEM((2, recycle_c.shape[0], dofs), BF16),
            pltpu.VMEM((blocks * blk, width), BF16),
            pltpu.VMEM((1, dofs), F32),
            pltpu.SMEM(pattern.shape, jnp.int32),
            pltpu.SMEM(send_list.shape, jnp.int32),
            pltpu.SMEM(part_sizes.shape, jnp.int32),
            pltpu.VMEM((2, wide, 16, LANES), F32),
            pltpu.VMEM((2, wide, 16, LANES), BF16),
            pltpu.VMEM((2, n_samp, wide, 16, LANES), BF16),
            pltpu.VMEM((wide, 16 * n_samp, LANES), F32),
            panel,
            panel,
            panel,
            pltpu.VMEM((cols, dofs), BF16),
            pltpu.VMEM((2 * cols, dofs), BF16),
            table,
            table,
            table,
            pltpu.VMEM((ITERS, 2, GHOST + GHOST // 2, 2 * cols, LANES), BF16),
            pltpu.VMEM((ITERS, 2, GHOST + GHOST // 2, 2 * cols, LANES), BF16),
            pltpu.VMEM((2, GHOST + GHOST // 2, recy, LANES), BF16),
            pltpu.VMEM((2, GHOST + GHOST // 2, recy, LANES), BF16),
            pltpu.VMEM((ITERS + 1, TILES, 8, LANES), F32),
            pltpu.VMEM((ITERS + 1, n_mesh, 8, LANES), F32),
            pltpu.VMEM((ITERS + 1, TILES, 8, LANES), F32),
            dma((8,)),
            dma((2,)),
            dma((2,)),
            dma((ITERS + 1, 2)),
            dma((ITERS + 1, 2)),
            dma((ITERS + 1,)),
            dma((ITERS + 1,)),
            dma((ITERS + 1,)),
            dma((ITERS + 1,)),
            dma((3,)),
        ],
        compiler_params=pltpu.CompilerParams(
            collective_id=0, has_side_effects=True, vmem_limit_bytes=56 << 20
        ),
    )(
        resid_in,
        recycle_u,
        recycle_c,
        stiff.reshape(blocks * blk, width),
        diag_scale.reshape(1, dofs),
        pattern,
        send_list,
        part_sizes,
    )


def solution(mesh):
    body = functools.partial(per_device, n_mesh=mesh.shape["mesh"], n_samp=mesh.shape["samp"])
    return jax.shard_map(
        body,
        mesh=mesh,
        in_specs=(
            P("samp", "mesh"),
            P("samp", "mesh"),
            P("samp", "mesh"),
            P("mesh", None, None),
            P("mesh"),
            P("mesh", None),
            P("mesh", None),
            P("mesh"),
        ),
        out_specs=(P("samp", "mesh"), P("samp", "mesh"), P(None, "samp")),
        check_vma=False,
    )
```

```python
import functools

import jax
import jax.numpy as jnp
from jax import lax
from jax.experimental import pallas as pl
from jax.experimental.pallas import tpu as pltpu
from jax.sharding import PartitionSpec as P

MESH = pl.DeviceIdType.MESH
F32 = jnp.float32
BF16 = jnp.bfloat16
LANES = 128
BLK = 192
PAIR = 2 * BLK
SLOTS = 6
GHOST = 8
ITERS = 2
TILES = 8


def nt(a, b):
    return lax.dot_general(a, b, (((1,), (1,)), ((), ())), preferred_element_type=F32)


def nn(a, b):
    return lax.dot_general(a, b, (((1,), (0,)), ((), ())), preferred_element_type=F32)


def split2(x):
    high = x.astype(BF16).astype(F32)
    return jnp.concatenate([high, x - high], 1).astype(BF16)


def halves(x):
    rows = x.shape[0] // 2
    return x[:rows] + x[rows:]


def turned(x):
    return pltpu.roll(x, LANES // 2, 1)


def kernel(
    n_mesh, n_samp,
    resid, u_in, c_in, stiff, diag, pattern_in, send_in, sizes_in,
    sol_out, res_out, coef_out,
    r, a, b, r_next, w_next,
    uc_loc, st, dg, pattern, send_list, sizes,
    stage, panel_send, panel_got, spread, cn, un, dn, rb, wb,
    t0, t1, r0t, send_f, got_f, send_c, got_c,
    pay, rs_got, ar_got,
    in_sems, panel_ssem, panel_rsem, ghost_ssem, ghost_rsem, rs_ssem, rs_rsem, ag_ssem, ag_rsem,
):
    me = lax.axis_index("mesh")
    mine = lax.axis_index("samp")
    cols, dofs = r.shape
    recy = cn.shape[0] // 2
    rows_per = recy // n_samp
    quarters = 16 // rows_per
    wide = dofs // quarters // LANES
    pairs = dofs // PAIR
    low_half = lax.broadcasted_iota(jnp.int32, (cols, LANES), 1) < LANES // 2
    highest = lax.Precision.HIGHEST

    loads = [
        pltpu.make_async_copy(src, dst, in_sems.at[i])
        for i, (src, dst) in enumerate(
            (
                (c_in, uc_loc.at[0]),
                (sizes_in, sizes),
                (resid, r),
                (send_in, send_list),
                (u_in, uc_loc.at[1]),
                (diag, dg),
                (pattern_in, pattern),
                (stiff, st),
            )
        )
    ]
    for load in loads:
        load.start()

    barrier = pltpu.get_barrier_semaphore()

    def greet_mesh(o, carry):
        pl.semaphore_signal(barrier, inc=1, device_id={"mesh": lax.rem(me + o, n_mesh)}, device_id_type=MESH)
        return carry

    def greet_samp(o, carry):
        pl.semaphore_signal(barrier, inc=1, device_id={"samp": lax.rem(mine + o, n_samp)}, device_id_type=MESH)
        return carry

    lax.fori_loop(1, n_mesh, greet_mesh, 0)
    lax.fori_loop(1, n_samp, greet_samp, 0)

    def row_alive(start, width):
        live = sizes[0] * BLK
        return (lax.broadcasted_iota(jnp.int32, (1, width), 1) + start) < live

    def pack_panel(which):
        local = uc_loc[which].astype(F32)
        for q in range(quarters):
            for t in range(wide):
                at = (q * wide + t) * LANES
                stage[which, t, pl.ds(q, rows_per, stride=quarters), :] = local[:, at : at + LANES]
        packed = stage[which].astype(BF16)
        panel_send[which] = packed
        panel_got[which, mine] = packed

    def send_panel(which):
        def one(o, carry):
            pltpu.make_async_remote_copy(
                src_ref=panel_send.at[which],
                dst_ref=panel_got.at[which, mine],
                send_sem=panel_ssem.at[which],
                recv_sem=panel_rsem.at[which],
                device_id={"samp": lax.rem(mine + o, n_samp)},
                device_id_type=MESH,
            ).start()
            return carry

        lax.fori_loop(1, n_samp, one, 0)

    def wait_panel(which, sems):
        others = panel_got.at[which, pl.ds(0, n_samp - 1)]
        pltpu.make_async_copy(others, others, sems.at[which]).wait()

    def natural(which, out):
        for k in range(n_samp):
            for t in range(wide):
                spread[t, 16 * k : 16 * k + 16, :] = panel_got[which, k, t].astype(F32)
        for q in range(quarters):
            for t in range(wide):
                at = (q * wide + t) * LANES
                tile = spread[t, pl.ds(q, recy, stride=quarters), :]
                tile = jnp.where(row_alive(at, LANES), tile, 0.0).astype(BF16)
                out[:recy, at : at + LANES] = tile
                out[recy:, at : at + LANES] = tile

    chips = n_mesh // 2
    span = chips // 2
    chip, core = lax.div(me, 2), lax.rem(me, 2)
    part = lax.rem(chip, span)
    reducer = core == lax.rem(part, 2)
    own_sum = lax.div(chip, span) * TILES + part
    all_sums = 2 * TILES

    def rs_send(which, value):
        for t in range(TILES):
            pay[which, t] = value[8 * t : 8 * t + 8, :]

        def one(t, carry):
            away = lax.rem(chip - t + chips + span // 2 - 1, chips)
            slot = 2 * lax.rem(away, span) + core
            target = 2 * lax.rem(t + span * lax.div(away, span), chips) + lax.rem(t, 2)

            @pl.when(target != me)
            def _():
                pltpu.make_async_remote_copy(
                    src_ref=pay.at[which, t],
                    dst_ref=rs_got.at[which, slot],
                    send_sem=rs_ssem.at[which],
                    recv_sem=rs_rsem.at[which],
                    device_id={"mesh": target},
                    device_id_type=MESH,
                ).start()

            @pl.when(target == me)
            def _():
                rs_got[which, slot] = pay[which, t]

            return carry

        lax.fori_loop(0, TILES, one, 0)

    def tiles_done(sem, count):
        some = ar_got.at[pl.ds(0, count)]
        pltpu.make_async_copy(some, some, sem).wait()

    def ag_send(which):
        @pl.when(reducer)
        def _():
            tiles_done(rs_rsem.at[which], 2 * span - 1)
            total = rs_got[which, 0]
            for d in range(1, 2 * span):
                total = total + rs_got[which, d]
            at = which * all_sums + own_sum
            ar_got[at] = total

            def one(o, carry):
                half = lax.div(o + 1, 2)
                ahead = n_mesh // 2 + half * (1 - 2 * lax.rem(o, 2))
                pltpu.make_async_remote_copy(
                    src_ref=ar_got.at[at],
                    dst_ref=ar_got.at[at],
                    send_sem=ag_ssem.at[which],
                    recv_sem=ag_rsem.at[which],
                    device_id={"mesh": lax.rem(me + ahead, n_mesh)},
                    device_id_type=MESH,
                ).start()
                return carry

            lax.fori_loop(0, n_mesh - 1, one, 0)

    def ar_wait(which):
        @pl.when(reducer)
        def _():
            tiles_done(ag_rsem.at[which], all_sums - 1)

        @pl.when(jnp.logical_not(reducer))
        def _():
            tiles_done(ag_rsem.at[which], all_sums)

        at = which * all_sums
        return jnp.concatenate([ar_got[at + t] + ar_got[at + TILES + t] for t in range(TILES)], 0)

    def ar_sent(which):
        @pl.when(reducer)
        def _():
            tiles_done(rs_ssem.at[which], TILES - 1)
            tiles_done(ag_ssem.at[which], n_mesh - 1)

        @pl.when(jnp.logical_not(reducer))
        def _():
            tiles_done(rs_ssem.at[which], TILES)

    def fill_tables(m, row, tiles):
        n0, n1, n2 = tiles
        b0, b1, b2 = n0.astype(BF16), n1.astype(BF16), n2.astype(BF16)
        v0, v1, v2 = turned(n0).astype(BF16), turned(n1).astype(BF16), turned(n2).astype(BF16)
        even, odd, rows = 2 * m, 2 * m + 1, slice(row, row + cols)
        t0[even, rows] = b0
        r0t[even, rows] = v0
        t1[even, rows] = jnp.where(low_half, b1, v1)
        t0[odd, rows] = jnp.where(low_half, v1, v2)
        r0t[odd, rows] = jnp.where(low_half, b2, b1)
        t1[odd, rows] = jnp.where(low_half, v2, b2)

    def fill_split(source):
        def one(m, carry):
            at = pl.multiple_of(m * PAIR, PAIR)
            tiles = [source[:, pl.ds(at + j * LANES, LANES)] for j in range(3)]
            fill_tables(m, 0, tiles)
            fill_tables(m, cols, [x - x.astype(BF16).astype(F32) for x in tiles])
            return carry

        lax.fori_loop(0, pairs, one, 0)

    def ghost_copies(send, got, which):
        out = []
        for side, by in ((0, 1), (1, n_mesh - 1)):
            out.append(
                pltpu.make_async_remote_copy(
                    src_ref=send.at[side],
                    dst_ref=got.at[side],
                    send_sem=ghost_ssem.at[which, side],
                    recv_sem=ghost_rsem.at[which, side],
                    device_id={"mesh": lax.rem(me + by, n_mesh)},
                    device_id_type=MESH,
                )
            )
        return out

    def pack_ghosts(send, row, rows):
        ends = (me == n_mesh - 1, me == 0)
        for side in range(2):
            keep = jnp.where(ends[side], 0.0, 1.0).astype(BF16)
            for start in range(0, rows, cols):
                span, to = slice(row + start, row + start + cols), slice(start, start + cols)
                for pair in range(GHOST // 2):
                    x, y = send_list[side, 2 * pair], send_list[side, 2 * pair + 1]
                    send[side, 2 * pair, to] = t0[x, span] * keep
                    send[side, 2 * pair + 1, to] = t0[y, span] * keep
                    send[side, GHOST + pair, to] = jnp.where(low_half, t1[x, span], t1[y, span]) * keep

    def take_ghosts(got, row, rows):
        for side in range(2):
            base = 2 * pairs + side * GHOST
            for start in range(0, rows, cols):
                span, to = slice(start, start + cols), slice(row + start, row + start + cols)
                for pair in range(GHOST // 2):
                    for j in range(2):
                        x = got[side, 2 * pair + j, span]
                        t0[base + 2 * pair + j, to] = x
                        r0t[base + 2 * pair + j, to] = turned(x.astype(F32)).astype(BF16)
                    x = got[side, GHOST + pair, span]
                    y = turned(x.astype(F32)).astype(BF16)
                    t1[base + 2 * pair, to] = jnp.where(low_half, x, y)
                    t1[base + 2 * pair + 1, to] = jnp.where(low_half, y, x)

    def apply_stiff(rows, emit):
        low_rows = lax.broadcasted_iota(jnp.int32, (rows, LANES), 1) < LANES // 2

        def gathered(i):
            parts = []
            for s in range(0, SLOTS, 2):
                x, y = pattern[s, i], pattern[s + 1, i]
                turned_y = r0t[y, :rows]
                parts.append(t0[x, :rows])
                parts.append(jnp.where(low_rows, t1[x, :rows], turned_y))
                parts.append(jnp.where(low_rows, turned_y, t1[y, :rows]))
            return jnp.concatenate(parts, 1)

        def one(m, carry):
            at = pl.multiple_of(m * PAIR, PAIR)
            out0 = nt(gathered(2 * m), st[pl.ds(at, 2 * LANES), :])
            out1 = nt(gathered(2 * m + 1), st[pl.ds(at + LANES, 2 * LANES), :])
            emit(at, 0, out0[:, :LANES])
            emit(at, 1, jnp.where(low_rows, out0[:, LANES:], out1[:, :LANES]))
            emit(at, 2, out1[:, LANES:])
            return carry

        lax.fori_loop(0, pairs, one, 0)

    def emit_first(at, j, value):
        span = pl.ds(at + j * LANES, LANES)
        keep, scale = row_alive(at + j * LANES, LANES), dg[:, span]
        a[:, span] = jnp.where(keep, halves(value[: 2 * cols]) + scale * r[:, span], 0.0)
        image = value[2 * cols :] + scale * cn[:recy, span].astype(F32)
        image = jnp.where(keep, image, 0.0).astype(BF16)
        dn[:recy, span] = image
        dn[recy:, span] = image

    def emit_second(at, j, value):
        span = pl.ds(at + j * LANES, LANES)
        b[:, span] = jnp.where(
            row_alive(at + j * LANES, LANES), halves(value) + dg[:, span] * a[:, span], 0.0
        )

    def renew(make, r_to, w_to):
        def one(m, carry):
            ww, wr = carry
            at = pl.multiple_of(m * PAIR, PAIR)
            span = pl.ds(at, PAIR)
            new_r, image = make(span)
            r_to[:, span] = new_r
            w_to[:, span] = image
            high = image.astype(BF16)
            wb[:cols, span] = high
            wb[cols:, span] = (image - high.astype(F32)).astype(BF16)
            for j in range(3):
                x = image[:, j * LANES : (j + 1) * LANES]
                ww = ww + x * x
                wr = wr + x * new_r[:, j * LANES : (j + 1) * LANES]
            return ww, wr

        zero = jnp.zeros((cols, LANES), F32)
        ww, wr = lax.fori_loop(0, pairs, one, (zero, zero), unroll=4)
        proj = halves(nt(wb[...], cn[:recy]))
        ww = jnp.sum(ww, axis=1, keepdims=True)
        wr = jnp.sum(wr, axis=1, keepdims=True)
        lane = lax.broadcasted_iota(jnp.int32, (cols, LANES - recy), 1)
        return jnp.concatenate([proj, jnp.where(lane == 0, ww, jnp.where(lane == 1, wr, 0.0))], 1)

    def step_of(reduced, c_r):
        proj = reduced[:, :recy]
        ww = reduced[:, recy : recy + 1]
        wr = reduced[:, recy + 1 : recy + 2]
        p_gram = jnp.dot(proj, gram, precision=highest, preferred_element_type=F32)
        bottom = ww + jnp.sum(proj * (p_gram - 2.0 * proj), axis=1, keepdims=True)
        top = wr - jnp.sum(proj * c_r, axis=1, keepdims=True)
        step = top / bottom
        return proj, step, c_r - step * (proj - p_gram)

    loads[0].wait()
    pack_panel(0)
    loads[1].wait()
    loads[2].wait()

    def mask(m, carry):
        at = pl.multiple_of(m * PAIR, PAIR)
        span = pl.ds(at, PAIR)
        kept = jnp.where(row_alive(at, PAIR), r[:, span], 0.0)
        r[:, span] = kept
        rb[:, span] = kept.astype(BF16)
        return carry

    lax.fori_loop(0, pairs, mask, 0)
    fill_split(r)
    loads[3].wait()
    pack_ghosts(send_f.at[0], 0, 2 * cols)
    loads[4].wait()
    pack_panel(1)
    pl.semaphore_wait(barrier, n_mesh + n_samp - 2)
    send_panel(0)
    for copy in ghost_copies(send_f.at[0], got_f.at[0], 0):
        copy.start()
    wait_panel(0, panel_rsem)
    natural(0, cn)
    first = nt(jnp.concatenate([rb[...], cn[:recy]], 0), cn[:recy])
    rs_send(0, jnp.concatenate([first[:cols], first[cols:]], 1))

    send_panel(1)
    def fill_panel(m, carry):
        at = pl.multiple_of(m * PAIR, PAIR)
        fill_tables(m, 2 * cols, [cn[:recy, pl.ds(at + j * LANES, LANES)].astype(F32) for j in range(3)])
        return carry

    lax.fori_loop(0, pairs, fill_panel, 0)
    pack_ghosts(send_c, 2 * cols, recy)
    for copy in ghost_copies(send_c, got_c, 1):
        copy.start()
    for copy in ghost_copies(send_f.at[0], got_f.at[0], 0):
        copy.wait()
    take_ghosts(got_f.at[0], 0, 2 * cols)
    for load in loads[5:]:
        load.wait()
    ag_send(0)
    for copy in ghost_copies(send_c, got_c, 1):
        copy.wait()
    take_ghosts(got_c, 2 * cols, recy)
    apply_stiff(2 * cols + recy, emit_first)
    reduced = ar_wait(0)
    coef = reduced[:, :recy]
    gram = reduced[:, recy:]
    coef2 = split2(coef)

    def make_first(span):
        new_r = r[:, span] - nn(coef2, cn[:, span])
        return new_r, a[:, span] - nn(coef2, dn[:, span])

    rs_send(1, renew(make_first, r, a))

    coef_out[...] = coef.T
    c_r = coef - jnp.dot(coef, gram, precision=highest, preferred_element_type=F32)
    fill_split(a)
    pack_ghosts(send_f.at[1], 0, 2 * cols)
    for copy in ghost_copies(send_f.at[1], got_f.at[1], 2):
        copy.start()
    wait_panel(1, panel_rsem)
    natural(1, un)
    ag_send(1)
    for copy in ghost_copies(send_f.at[1], got_f.at[1], 2):
        copy.wait()
    take_ghosts(got_f.at[1], 0, 2 * cols)
    apply_stiff(2 * cols, emit_second)
    proj, step1, c_r = step_of(ar_wait(1), c_r)
    proj2 = split2(proj)

    def make_second(span):
        image = a[:, span]
        new_r = r[:, span] - step1 * (image - nn(proj2, cn[:, span]))
        return new_r, image - step1 * (b[:, span] - nn(proj2, dn[:, span]))

    rs_send(2, renew(make_second, r_next, w_next))

    carried2 = split2(coef - step1 * proj)

    def base(m, carry):
        span = pl.ds(pl.multiple_of(m * PAIR, PAIR), PAIR)
        rounded = r[:, span].astype(BF16).astype(F32)
        sol_out[:, span] = nn(carried2, un[:, span]) + step1 * rounded
        return carry

    lax.fori_loop(0, pairs, base, 0, unroll=2)
    ag_send(2)
    proj, step2, _ = step_of(ar_wait(2), c_r)
    proj2 = split2(proj)

    def finish(m, carry):
        span = pl.ds(pl.multiple_of(m * PAIR, PAIR), PAIR)
        old = r_next[:, span]
        res_out[:, span] = old - step2 * (w_next[:, span] - nn(proj2, cn[:, span]))
        rounded = old.astype(BF16).astype(F32)
        sol_out[:, span] = sol_out[:, span] + step2 * (rounded - nn(proj2, un[:, span]))
        return carry

    lax.fori_loop(0, pairs, finish, 0, unroll=4)
    for which in range(ITERS + 1):
        ar_sent(which)
    for which in range(2):
        wait_panel(which, panel_ssem)


def per_device(resid_in, recycle_u, recycle_c, stiff, diag_scale, pattern, send_list, part_sizes, n_mesh, n_samp):
    cols, dofs = resid_in.shape
    blocks, blk, width = stiff.shape
    recy = recycle_c.shape[0] * n_samp
    wide = dofs * recycle_c.shape[0] // 16 // LANES
    ext = blocks + 2 * GHOST
    hbm = pl.BlockSpec(memory_space=pltpu.HBM)
    vmem = pl.BlockSpec(memory_space=pltpu.VMEM)
    dma = pltpu.SemaphoreType.DMA
    field = pltpu.VMEM((cols, dofs), F32)
    panel = pltpu.VMEM((2 * recy, dofs), BF16)
    table = pltpu.VMEM((ext, 2 * cols + recy, LANES), BF16)
    return pl.pallas_call(
        functools.partial(kernel, n_mesh, n_samp),
        out_shape=(
            jax.ShapeDtypeStruct((cols, dofs), F32),
            jax.ShapeDtypeStruct((cols, dofs), F32),
            jax.ShapeDtypeStruct((recy, cols), F32),
        ),
        in_specs=[hbm] * 8,
        out_specs=(vmem, vmem, vmem),
        scratch_shapes=[
            field,
            field,
            field,
            field,
            field,
            pltpu.VMEM((2, recycle_c.shape[0], dofs), BF16),
            pltpu.VMEM((blocks * blk, width), BF16),
            pltpu.VMEM((1, dofs), F32),
            pltpu.SMEM(pattern.shape[::-1], jnp.int32),
            pltpu.SMEM(send_list.shape, jnp.int32),
            pltpu.SMEM(part_sizes.shape, jnp.int32),
            pltpu.VMEM((2, wide, 16, LANES), F32),
            pltpu.VMEM((2, wide, 16, LANES), BF16),
            pltpu.VMEM((2, n_samp, wide, 16, LANES), BF16),
            pltpu.VMEM((wide, 16 * n_samp, LANES), F32),
            panel,
            panel,
            panel,
            pltpu.VMEM((cols, dofs), BF16),
            pltpu.VMEM((2 * cols, dofs), BF16),
            table,
            table,
            table,
            pltpu.VMEM((ITERS, 2, GHOST + GHOST // 2, 2 * cols, LANES), BF16),
            pltpu.VMEM((ITERS, 2, GHOST + GHOST // 2, 2 * cols, LANES), BF16),
            pltpu.VMEM((2, GHOST + GHOST // 2, recy, LANES), BF16),
            pltpu.VMEM((2, GHOST + GHOST // 2, recy, LANES), BF16),
            pltpu.VMEM((ITERS + 1, TILES, 8, LANES), F32),
            pltpu.VMEM((ITERS + 1, n_mesh // 2, 8, LANES), F32),
            pltpu.VMEM(((ITERS + 1) * 2 * TILES, 8, LANES), F32),
            dma((8,)),
            dma((2,)),
            dma((2,)),
            dma((ITERS + 1, 2)),
            dma((ITERS + 1, 2)),
            dma((ITERS + 1,)),
            dma((ITERS + 1,)),
            dma((ITERS + 1,)),
            dma((ITERS + 1,)),
        ],
        compiler_params=pltpu.CompilerParams(
            collective_id=0, has_side_effects=True, vmem_limit_bytes=62 << 20
        ),
    )(
        resid_in,
        recycle_u,
        recycle_c,
        stiff.reshape(blocks * blk, width),
        diag_scale.reshape(1, dofs),
        pattern.T,
        send_list,
        part_sizes,
    )


def solution(mesh):
    body = functools.partial(per_device, n_mesh=mesh.shape["mesh"], n_samp=mesh.shape["samp"])
    return jax.shard_map(
        body,
        mesh=mesh,
        in_specs=(
            P("samp", "mesh"),
            P("samp", "mesh"),
            P("samp", "mesh"),
            P("mesh", None, None),
            P("mesh"),
            P("mesh", None),
            P("mesh", None),
            P("mesh"),
        ),
        out_specs=(P("samp", "mesh"), P("samp", "mesh"), P(None, "samp")),
        check_vma=False,
    )
```

```python
import functools

import jax
import jax.numpy as jnp
from jax import lax
from jax.experimental import pallas as pl
from jax.experimental.pallas import tpu as pltpu
from jax.sharding import PartitionSpec as P

MESH = pl.DeviceIdType.MESH
F32 = jnp.float32
BF16 = jnp.bfloat16
LANES = 128
BLK = 192
PAIR = 2 * BLK
SLOTS = 6
GHOST = 8
ITERS = 2
TILES = 8
REACH = 4
PARTS = 4


def nt(a, b):
    return lax.dot_general(a, b, (((1,), (1,)), ((), ())), preferred_element_type=F32)


def nn(a, b):
    return lax.dot_general(a, b, (((1,), (0,)), ((), ())), preferred_element_type=F32)


def split2(x):
    high = x.astype(BF16).astype(F32)
    return jnp.concatenate([high, x - high], 1).astype(BF16)


def halves(x):
    rows = x.shape[0] // 2
    return x[:rows] + x[rows:]


def turned(x):
    return pltpu.roll(x, LANES // 2, 1)


def kernel(
    n_mesh, n_samp,
    resid, u_in, c_in, stiff, diag, pattern_in, send_in, sizes_in,
    r_out, w_out, base_out, cn_out, un_out, fin_out, coef_out,
    r, a, b, r_next, w_next, base_sol, fin, coef_t, own,
    uc_loc, st, dg, pattern, send_list, sizes,
    stage, panel_send, panel_got, spread, cn, un, dn, rb, wb,
    t0, t1, r0t, send_f, got_f, send_c, got_c,
    pay, rs_got, ar_got,
    in_sems, panel_ssem, panel_rsem, ghost_ssem, ghost_rsem, rs_ssem, rs_rsem, ag_ssem, ag_rsem, out_sems, far_sem,
):
    me = lax.axis_index("mesh")
    mine = lax.axis_index("samp")
    cols, dofs = r.shape
    recy = cn.shape[0] // 2
    rows_per = recy // n_samp
    quarters = 16 // rows_per
    wide = dofs // quarters // LANES
    pairs = dofs // PAIR
    low_half = lax.broadcasted_iota(jnp.int32, (cols, LANES), 1) < LANES // 2
    highest = lax.Precision.HIGHEST

    loads = [
        pltpu.make_async_copy(src, dst, in_sems.at[i])
        for i, (src, dst) in enumerate(
            (
                (c_in, uc_loc.at[0]),
                (sizes_in, sizes),
                (resid, r),
                (send_in, send_list),
                (u_in, uc_loc.at[1]),
                (diag, dg),
                (pattern_in, pattern),
                (stiff, st),
            )
        )
    ]
    for load in loads:
        load.start()

    barrier = pltpu.get_barrier_semaphore()
    chips = n_mesh // 2
    chip, core = lax.div(me, 2), lax.rem(me, 2)

    def greet_mesh(o, carry):
        peer = 2 * lax.rem(chip + chips - REACH + lax.div(o, 2), chips) + lax.rem(o, 2)

        @pl.when(peer != me)
        def _():
            pl.semaphore_signal(barrier, inc=1, device_id={"mesh": peer}, device_id_type=MESH)

        return carry

    def greet_samp(o, carry):
        pl.semaphore_signal(barrier, inc=1, device_id={"samp": lax.rem(mine + o, n_samp)}, device_id_type=MESH)
        return carry

    lax.fori_loop(0, 4 * REACH + 2, greet_mesh, 0)
    lax.fori_loop(1, n_samp, greet_samp, 0)

    def row_alive(start, width):
        live = sizes[0] * BLK
        return (lax.broadcasted_iota(jnp.int32, (1, width), 1) + start) < live

    def pack_panel(which):
        local = uc_loc[which].astype(F32)
        for q in range(quarters):
            for t in range(wide):
                at = (q * wide + t) * LANES
                stage[which, t, pl.ds(q, rows_per, stride=quarters), :] = local[:, at : at + LANES]
        packed = stage[which].astype(BF16)
        panel_send[which] = packed
        panel_got[which, mine] = packed

    def send_panel(which):
        def one(o, carry):
            pltpu.make_async_remote_copy(
                src_ref=panel_send.at[which],
                dst_ref=panel_got.at[which, mine],
                send_sem=panel_ssem.at[which],
                recv_sem=panel_rsem.at[which],
                device_id={"samp": lax.rem(mine + o, n_samp)},
                device_id_type=MESH,
            ).start()
            return carry

        lax.fori_loop(1, n_samp, one, 0)

    def wait_panel(which, sems):
        others = panel_got.at[which, pl.ds(0, n_samp - 1)]
        pltpu.make_async_copy(others, others, sems.at[which]).wait()

    def natural(which, out):
        for k in range(n_samp):
            for t in range(wide):
                spread[t, 16 * k : 16 * k + 16, :] = panel_got[which, k, t].astype(F32)
        for q in range(quarters):
            for t in range(wide):
                at = (q * wide + t) * LANES
                tile = spread[t, pl.ds(q, recy, stride=quarters), :]
                tile = jnp.where(row_alive(at, LANES), tile, 0.0).astype(BF16)
                out[:recy, at : at + LANES] = tile
                out[recy:, at : at + LANES] = tile

    span = chips // 2
    part = lax.rem(chip, span)
    reducer = core == lax.rem(part, 2)
    own_sum = lax.div(chip, span) * TILES + part
    all_sums = 2 * TILES

    def rs_send(which, value):
        for t in range(TILES):
            pay[which, t] = value[8 * t : 8 * t + 8, :]

        def one(t, carry):
            away = lax.rem(chip - t + chips + span // 2 - 1, chips)
            slot = 2 * lax.rem(away, span) + core
            target = 2 * lax.rem(t + span * lax.div(away, span), chips) + lax.rem(t, 2)

            @pl.when(target != me)
            def _():
                pltpu.make_async_remote_copy(
                    src_ref=pay.at[which, t],
                    dst_ref=rs_got.at[which, slot],
                    send_sem=rs_ssem.at[which],
                    recv_sem=rs_rsem.at[which],
                    device_id={"mesh": target},
                    device_id_type=MESH,
                ).start()

            @pl.when(target == me)
            def _():
                rs_got[which, slot] = pay[which, t]

            return carry

        lax.fori_loop(0, TILES, one, 0)

    def tiles_done(sem, count):
        some = ar_got.at[pl.ds(0, count)]
        pltpu.make_async_copy(some, some, sem).wait()

    def ag_send(which):
        @pl.when(reducer)
        def _():
            tiles_done(rs_rsem.at[which], 2 * span - 1)
            total = rs_got[which, 0]
            for d in range(1, 2 * span):
                total = total + rs_got[which, d]
            at = which * all_sums + own_sum
            ar_got[at] = total

            def one(o, carry):
                half = lax.div(o + 1, 2)
                ahead = n_mesh // 2 + half * (1 - 2 * lax.rem(o, 2))
                pltpu.make_async_remote_copy(
                    src_ref=ar_got.at[at],
                    dst_ref=ar_got.at[at],
                    send_sem=ag_ssem.at[which],
                    recv_sem=ag_rsem.at[which],
                    device_id={"mesh": lax.rem(me + ahead, n_mesh)},
                    device_id_type=MESH,
                ).start()
                return carry

            lax.fori_loop(0, n_mesh - 1, one, 0)

    def ar_wait(which):
        @pl.when(reducer)
        def _():
            tiles_done(ag_rsem.at[which], all_sums - 1)

        @pl.when(jnp.logical_not(reducer))
        def _():
            tiles_done(ag_rsem.at[which], all_sums)

        at = which * all_sums
        return jnp.concatenate([ar_got[at + t] + ar_got[at + TILES + t] for t in range(TILES)], 0)

    def ar_sent(which):
        @pl.when(reducer)
        def _():
            tiles_done(rs_ssem.at[which], TILES - 1)
            tiles_done(ag_ssem.at[which], n_mesh - 1)

        @pl.when(jnp.logical_not(reducer))
        def _():
            tiles_done(rs_ssem.at[which], TILES)

    def fill_tables(m, row, tiles):
        n0, n1, n2 = tiles
        b0, b1, b2 = n0.astype(BF16), n1.astype(BF16), n2.astype(BF16)
        v0, v1, v2 = turned(n0).astype(BF16), turned(n1).astype(BF16), turned(n2).astype(BF16)
        even, odd, rows = 2 * m, 2 * m + 1, slice(row, row + cols)
        t0[even, rows] = b0
        r0t[even, rows] = v0
        t1[even, rows] = jnp.where(low_half, b1, v1)
        t0[odd, rows] = jnp.where(low_half, v1, v2)
        r0t[odd, rows] = jnp.where(low_half, b2, b1)
        t1[odd, rows] = jnp.where(low_half, v2, b2)

    def fill_split(source):
        def one(m, carry):
            at = pl.multiple_of(m * PAIR, PAIR)
            tiles = [source[:, pl.ds(at + j * LANES, LANES)] for j in range(3)]
            fill_tables(m, 0, tiles)
            fill_tables(m, cols, [x - x.astype(BF16).astype(F32) for x in tiles])
            return carry

        lax.fori_loop(0, pairs, one, 0)

    def ghost_copies(send, got, which):
        out = []
        for side, by in ((0, 1), (1, n_mesh - 1)):
            out.append(
                pltpu.make_async_remote_copy(
                    src_ref=send.at[side],
                    dst_ref=got.at[side],
                    send_sem=ghost_ssem.at[which, side],
                    recv_sem=ghost_rsem.at[which, side],
                    device_id={"mesh": lax.rem(me + by, n_mesh)},
                    device_id_type=MESH,
                )
            )
        return out

    def pack_ghosts(send, row, rows, copies=()):
        ends = (me == n_mesh - 1, me == 0)
        for side in range(2):
            keep = jnp.where(ends[side], 0.0, 1.0).astype(BF16)
            for start in range(0, rows, cols):
                span, to = slice(row + start, row + start + cols), slice(start, start + cols)
                for pair in range(GHOST // 2):
                    x, y = send_list[side, 2 * pair], send_list[side, 2 * pair + 1]
                    send[side, 2 * pair, to] = t0[x, span] * keep
                    send[side, 2 * pair + 1, to] = t0[y, span] * keep
                    send[side, GHOST + pair, to] = jnp.where(low_half, t1[x, span], t1[y, span]) * keep
            if copies:
                copies[side].start()

    def take_ghosts(got, row, rows):
        for side in range(2):
            base = 2 * pairs + side * GHOST
            for start in range(0, rows, cols):
                span, to = slice(start, start + cols), slice(row + start, row + start + cols)
                for pair in range(GHOST // 2):
                    for j in range(2):
                        x = got[side, 2 * pair + j, span]
                        t0[base + 2 * pair + j, to] = x
                        r0t[base + 2 * pair + j, to] = turned(x.astype(F32)).astype(BF16)
                    x = got[side, GHOST + pair, span]
                    y = turned(x.astype(F32)).astype(BF16)
                    t1[base + 2 * pair, to] = jnp.where(low_half, x, y)
                    t1[base + 2 * pair + 1, to] = jnp.where(low_half, y, x)

    def by_pairs(rows, low_rows, lanes, left, emit):
        def one(m, carry):
            at = pl.multiple_of(m * PAIR, PAIR)
            out0 = nt(left(2 * m), st[pl.ds(at, 2 * LANES), lanes])
            out1 = nt(left(2 * m + 1), st[pl.ds(at + LANES, 2 * LANES), lanes])
            emit(at, 0, out0[:, :LANES])
            emit(at, 1, jnp.where(low_rows, out0[:, LANES:], out1[:, :LANES]))
            emit(at, 2, out1[:, LANES:])
            return carry

        lax.fori_loop(0, pairs, one, 0)

    def apply_own(rows):
        low_rows = lax.broadcasted_iota(jnp.int32, (rows, LANES), 1) < LANES // 2
        none = jnp.zeros((rows, LANES), BF16)

        def left(i):
            return jnp.concatenate([t0[i, :rows], jnp.where(low_rows, t1[i, :rows], none)], 1)

        def emit(at, j, value):
            own[:rows, pl.ds(at + j * LANES, LANES)] = value

        by_pairs(rows, low_rows, slice(0, 2 * LANES), left, emit)

    def apply_stiff(rows, emit):
        low_rows = lax.broadcasted_iota(jnp.int32, (rows, LANES), 1) < LANES // 2
        none = jnp.zeros((rows, LANES), BF16)

        def left(i):
            parts = []
            for s in range(0, SLOTS, 2):
                x, y = pattern[s, i], pattern[s + 1, i]
                turned_y = r0t[y, :rows]
                if s:
                    parts.append(t0[x, :rows])
                parts.append(jnp.where(low_rows, t1[x, :rows] if s else none, turned_y))
                parts.append(jnp.where(low_rows, turned_y, t1[y, :rows]))
            return jnp.concatenate(parts, 1)

        def whole(at, j, value):
            emit(at, j, value + own[:rows, pl.ds(at + j * LANES, LANES)])

        by_pairs(rows, low_rows, slice(LANES, SLOTS * BLK), left, whole)

    def emit_first(at, j, value):
        span = pl.ds(at + j * LANES, LANES)
        keep, scale = row_alive(at + j * LANES, LANES), dg[:, span]
        a[:, span] = jnp.where(keep, halves(value[: 2 * cols]) + scale * r[:, span], 0.0)
        image = value[2 * cols :] + scale * cn[:recy, span].astype(F32)
        image = jnp.where(keep, image, 0.0).astype(BF16)
        dn[:recy, span] = image
        dn[recy:, span] = image

    def emit_second(at, j, value):
        span = pl.ds(at + j * LANES, LANES)
        b[:, span] = jnp.where(
            row_alive(at + j * LANES, LANES), halves(value) + dg[:, span] * a[:, span], 0.0
        )

    def renew(make, r_to, w_to):
        def one(m, carry):
            ww, wr = carry
            at = pl.multiple_of(m * PAIR, PAIR)
            span = pl.ds(at, PAIR)
            new_r, image = make(span)
            r_to[:, span] = new_r
            w_to[:, span] = image
            high = image.astype(BF16)
            wb[:cols, span] = high
            wb[cols:, span] = (image - high.astype(F32)).astype(BF16)
            for j in range(3):
                x = image[:, j * LANES : (j + 1) * LANES]
                ww = ww + x * x
                wr = wr + x * new_r[:, j * LANES : (j + 1) * LANES]
            return ww, wr

        zero = jnp.zeros((cols, LANES), F32)
        ww, wr = lax.fori_loop(0, pairs, one, (zero, zero), unroll=4)
        proj = halves(nt(wb[...], cn[:recy]))
        ww = jnp.sum(ww, axis=1, keepdims=True)
        wr = jnp.sum(wr, axis=1, keepdims=True)
        lane = lax.broadcasted_iota(jnp.int32, (cols, LANES - recy), 1)
        return jnp.concatenate([proj, jnp.where(lane == 0, ww, jnp.where(lane == 1, wr, 0.0))], 1)

    def step_of(reduced, c_r):
        proj = reduced[:, :recy]
        ww = reduced[:, recy : recy + 1]
        wr = reduced[:, recy + 1 : recy + 2]
        p_gram = jnp.dot(proj, gram, precision=highest, preferred_element_type=F32)
        bottom = ww + jnp.sum(proj * (p_gram - 2.0 * proj), axis=1, keepdims=True)
        top = wr - jnp.sum(proj * c_r, axis=1, keepdims=True)
        step = top / bottom
        return proj, step, c_r - step * (proj - p_gram)

    loads[0].wait()
    pack_panel(0)
    loads[1].wait()
    loads[2].wait()

    def mask(m, carry):
        at = pl.multiple_of(m * PAIR, PAIR)
        span = pl.ds(at, PAIR)
        kept = jnp.where(row_alive(at, PAIR), r[:, span], 0.0)
        r[:, span] = kept
        rb[:, span] = kept.astype(BF16)
        return carry

    lax.fori_loop(0, pairs, mask, 0)
    fill_split(r)
    loads[3].wait()
    pack_ghosts(send_f.at[0], 0, 2 * cols)
    loads[4].wait()
    pack_panel(1)
    pl.semaphore_wait(barrier, 4 * REACH + n_samp)
    for by in (REACH, chips - REACH):
        peer = 2 * lax.rem(chip + by, chips) + core
        pl.semaphore_signal(far_sem, inc=1, device_id={"mesh": peer}, device_id_type=MESH)
    send_panel(0)
    for copy in ghost_copies(send_f.at[0], got_f.at[0], 0):
        copy.start()
    wait_panel(0, panel_rsem)
    natural(0, cn)
    first = nt(jnp.concatenate([rb[...], cn[:recy]], 0), cn[:recy])
    rs_send(0, jnp.concatenate([first[:cols], first[cols:]], 1))

    send_panel(1)
    def fill_panel(m, carry):
        at = pl.multiple_of(m * PAIR, PAIR)
        fill_tables(m, 2 * cols, [cn[:recy, pl.ds(at + j * LANES, LANES)].astype(F32) for j in range(3)])
        return carry

    lax.fori_loop(0, pairs, fill_panel, 0)
    pack_ghosts(send_c, 2 * cols, recy, ghost_copies(send_c, got_c, 1))
    for copy in ghost_copies(send_f.at[0], got_f.at[0], 0):
        copy.wait()
    take_ghosts(got_f.at[0], 0, 2 * cols)
    for load in loads[5:]:
        load.wait()
    apply_own(2 * cols + recy)
    pl.semaphore_wait(far_sem, 2)
    ag_send(0)
    for copy in ghost_copies(send_c, got_c, 1):
        copy.wait()
    take_ghosts(got_c, 2 * cols, recy)
    apply_stiff(2 * cols + recy, emit_first)
    reduced = ar_wait(0)
    coef = reduced[:, :recy]
    gram = reduced[:, recy:]
    coef2 = split2(coef)

    def make_first(span):
        new_r = r[:, span] - nn(coef2, cn[:, span])
        return new_r, a[:, span] - nn(coef2, dn[:, span])

    rs_send(1, renew(make_first, r, a))

    coef_t[...] = coef.T
    c_r = coef - jnp.dot(coef, gram, precision=highest, preferred_element_type=F32)
    fill_split(a)
    pack_ghosts(send_f.at[1], 0, 2 * cols, ghost_copies(send_f.at[1], got_f.at[1], 2))
    apply_own(2 * cols)
    wait_panel(1, panel_rsem)
    natural(1, un)
    ag_send(1)
    for copy in ghost_copies(send_f.at[1], got_f.at[1], 2):
        copy.wait()
    take_ghosts(got_f.at[1], 0, 2 * cols)
    apply_stiff(2 * cols, emit_second)
    proj, step1, c_r = step_of(ar_wait(1), c_r)
    proj2 = split2(proj)

    def make_second(span):
        image = a[:, span]
        new_r = r[:, span] - step1 * (image - nn(proj2, cn[:, span]))
        return new_r, image - step1 * (b[:, span] - nn(proj2, dn[:, span]))

    rs_send(2, renew(make_second, r_next, w_next))

    carried2 = split2(coef - step1 * proj)

    def base(m, carry):
        span = pl.ds(pl.multiple_of(m * PAIR, PAIR), PAIR)
        rounded = r[:, span].astype(BF16).astype(F32)
        base_sol[:, span] = nn(carried2, un[:, span]) + step1 * rounded
        return carry

    lax.fori_loop(0, pairs, base, 0, unroll=2)
    outs = [
        pltpu.make_async_copy(src, dst, out_sems.at[i])
        for i, (src, dst) in enumerate(
            (
                (r_next, r_out),
                (w_next, w_out),
                (base_sol, base_out),
                (cn.at[:recy], cn_out),
                (un.at[:recy], un_out),
                (coef_t, coef_out),
                (fin, fin_out),
            )
        )
    ]
    for copy in outs[:6]:
        copy.start()
    for which in range(2):
        wait_panel(which, panel_ssem)
        ar_sent(which)
    ag_send(2)
    proj, step2, _ = step_of(ar_wait(2), c_r)
    fin[...] = jnp.concatenate([proj, jnp.broadcast_to(step2, (cols, LANES - recy))], 1)
    outs[6].start()
    ar_sent(2)
    for copy in outs:
        copy.wait()

def last_kernel(
    r_in, w_in, base_in, cn_in, un_in, fin_in, coef_in,
    sol_out, res_out, coef_out,
    r, w, sol, cn, un, fin, in_sems, out_sems,
):
    cols, dofs = r.shape
    recy = cn.shape[0]
    width = dofs // PARTS
    coef_copy = pltpu.make_async_copy(coef_in, coef_out, out_sems.at[0, 0])
    coef_copy.start()
    fin_copy = pltpu.make_async_copy(fin_in, fin, out_sems.at[0, 1])
    fin_copy.start()
    loads, outs = [], []
    for i in range(PARTS):
        span = pl.ds(i * width, width)
        pairs = ((cn_in, cn), (w_in, w), (r_in, r), (un_in, un), (base_in, sol))
        loads.append(
            [
                pltpu.make_async_copy(src.at[:, span], dst.at[:, span], in_sems.at[i, j])
                for j, (src, dst) in enumerate(pairs)
            ]
        )
        for load in loads[-1]:
            load.start()
    fin_copy.wait()
    proj, step = fin[:, :recy], fin[:, recy : recy + 1]
    high = proj.astype(BF16)
    proj2 = jnp.concatenate([high, (proj - high.astype(F32)).astype(BF16)], 0)
    for i in range(PARTS):
        for load in loads[i]:
            load.wait()
        at = slice(i * width, (i + 1) * width)
        old = r[:, at]
        r[:, at] = old - step * (w[:, at] - halves(nn(proj2, cn[:, at])))
        rounded = old.astype(BF16).astype(F32)
        sol[:, at] = sol[:, at] + step * (rounded - halves(nn(proj2, un[:, at])))
        for j, (src, dst) in enumerate(((r, res_out), (sol, sol_out))):
            span = pl.ds(i * width, width)
            out = pltpu.make_async_copy(src.at[:, span], dst.at[:, span], out_sems.at[i + 1, j])
            out.start()
            outs.append(out)
    coef_copy.wait()
    for out in outs:
        out.wait()


def per_device(resid_in, recycle_u, recycle_c, stiff, diag_scale, pattern, send_list, part_sizes, n_mesh, n_samp):
    cols, dofs = resid_in.shape
    blocks, blk, width = stiff.shape
    recy = recycle_c.shape[0] * n_samp
    wide = dofs * recycle_c.shape[0] // 16 // LANES
    ext = blocks + 2 * GHOST
    hbm = pl.BlockSpec(memory_space=pltpu.HBM)
    dma = pltpu.SemaphoreType.DMA
    field = pltpu.VMEM((cols, dofs), F32)
    panel = pltpu.VMEM((2 * recy, dofs), BF16)
    table = pltpu.VMEM((ext, 2 * cols + recy, LANES), BF16)
    middle = pl.pallas_call(
        functools.partial(kernel, n_mesh, n_samp),
        out_shape=(
            jax.ShapeDtypeStruct((cols, dofs), F32),
            jax.ShapeDtypeStruct((cols, dofs), F32),
            jax.ShapeDtypeStruct((cols, dofs), F32),
            jax.ShapeDtypeStruct((recy, dofs), BF16),
            jax.ShapeDtypeStruct((recy, dofs), BF16),
            jax.ShapeDtypeStruct((cols, LANES), F32),
            jax.ShapeDtypeStruct((recy, cols), F32),
        ),
        in_specs=[hbm] * 8,
        out_specs=(hbm,) * 7,
        scratch_shapes=[
            field,
            field,
            field,
            field,
            field,
            field,
            pltpu.VMEM((cols, LANES), F32),
            pltpu.VMEM((recy, cols), F32),
            pltpu.VMEM((2 * cols + recy, dofs), F32),
            pltpu.VMEM((2, recycle_c.shape[0], dofs), BF16),
            pltpu.VMEM((blocks * blk, width), BF16),
            pltpu.VMEM((1, dofs), F32),
            pltpu.SMEM(pattern.shape[::-1], jnp.int32),
            pltpu.SMEM(send_list.shape, jnp.int32),
            pltpu.SMEM(part_sizes.shape, jnp.int32),
            pltpu.VMEM((2, wide, 16, LANES), F32),
            pltpu.VMEM((2, wide, 16, LANES), BF16),
            pltpu.VMEM((2, n_samp, wide, 16, LANES), BF16),
            pltpu.VMEM((wide, 16 * n_samp, LANES), F32),
            panel,
            panel,
            panel,
            pltpu.VMEM((cols, dofs), BF16),
            pltpu.VMEM((2 * cols, dofs), BF16),
            table,
            table,
            table,
            pltpu.VMEM((ITERS, 2, GHOST + GHOST // 2, 2 * cols, LANES), BF16),
            pltpu.VMEM((ITERS, 2, GHOST + GHOST // 2, 2 * cols, LANES), BF16),
            pltpu.VMEM((2, GHOST + GHOST // 2, recy, LANES), BF16),
            pltpu.VMEM((2, GHOST + GHOST // 2, recy, LANES), BF16),
            pltpu.VMEM((ITERS + 1, TILES, 8, LANES), F32),
            pltpu.VMEM((ITERS + 1, n_mesh // 2, 8, LANES), F32),
            pltpu.VMEM(((ITERS + 1) * 2 * TILES, 8, LANES), F32),
            dma((8,)),
            dma((2,)),
            dma((2,)),
            dma((ITERS + 1, 2)),
            dma((ITERS + 1, 2)),
            dma((ITERS + 1,)),
            dma((ITERS + 1,)),
            dma((ITERS + 1,)),
            dma((ITERS + 1,)),
            dma((7,)),
            pltpu.SemaphoreType.REGULAR,
        ],
        compiler_params=pltpu.CompilerParams(
            collective_id=0, has_side_effects=True, vmem_limit_bytes=62 << 20
        ),
    )(
        resid_in,
        recycle_u,
        recycle_c,
        stiff.reshape(blocks * blk, width),
        diag_scale.reshape(1, dofs),
        pattern.T,
        send_list,
        part_sizes,
    )
    plain = pltpu.VMEM((recy, dofs), BF16)
    return pl.pallas_call(
        last_kernel,
        out_shape=(
            jax.ShapeDtypeStruct((cols, dofs), F32),
            jax.ShapeDtypeStruct((cols, dofs), F32),
            jax.ShapeDtypeStruct((recy, cols), F32),
        ),
        in_specs=[hbm] * 7,
        out_specs=(hbm,) * 3,
        scratch_shapes=[
            field,
            field,
            field,
            plain,
            plain,
            pltpu.VMEM((cols, LANES), F32),
            dma((PARTS, 5)),
            dma((PARTS + 1, 2)),
        ],
        compiler_params=pltpu.CompilerParams(vmem_limit_bytes=62 << 20),
    )(*middle)


def solution(mesh):
    body = functools.partial(per_device, n_mesh=mesh.shape["mesh"], n_samp=mesh.shape["samp"])
    return jax.shard_map(
        body,
        mesh=mesh,
        in_specs=(
            P("samp", "mesh"),
            P("samp", "mesh"),
            P("samp", "mesh"),
            P("mesh", None, None),
            P("mesh"),
            P("mesh", None),
            P("mesh", None),
            P("mesh"),
        ),
        out_specs=(P("samp", "mesh"), P("samp", "mesh"), P(None, "samp")),
        check_vma=False,
    )
```

```python
import functools

import jax
import jax.numpy as jnp
from jax import lax
from jax.experimental import pallas as pl
from jax.experimental.pallas import tpu as pltpu
from jax.sharding import PartitionSpec as P

MESH = pl.DeviceIdType.MESH
F32 = jnp.float32
BF16 = jnp.bfloat16
LANES = 128
BLK = 192
PAIR = 2 * BLK
SLOTS = 6
GHOST = 8
ITERS = 2
TILES = 8
REACH = 4
SQUARE = 4
PARTS = 2


def nt(a, b):
    return lax.dot_general(a, b, (((1,), (1,)), ((), ())), preferred_element_type=F32)


def nn(a, b):
    return lax.dot_general(a, b, (((1,), (0,)), ((), ())), preferred_element_type=F32)


def split2(x):
    high = x.astype(BF16).astype(F32)
    return jnp.concatenate([high, x - high], 1).astype(BF16)


def halves(x):
    rows = x.shape[0] // 2
    return x[:rows] + x[rows:]


def turned(x):
    return pltpu.roll(x, LANES // 2, 1)


def kernel(
    n_mesh, n_samp,
    resid, u_in, c_in, stiff, diag, pattern_in, send_in, sizes_in,
    fields_out, panels_out, fin_out, coef_out,
    r, a, b, r_next, w_next, base_sol, fin, coef_t, own,
    uc_loc, st, dg, pattern, send_list, sizes,
    stage, panel_send, panel_got, spread, cn, un, dn, rb, wb,
    t0, t1, r0t, send_f, got_f, send_c, got_c,
    pay, rs_got, ar_got,
    in_sems, panel_ssem, panel_rsem, ghost_ssem, ghost_rsem, rs_ssem, rs_rsem, ag_ssem, ag_rsem, out_sems, far_sem,
):
    me = lax.axis_index("mesh")
    mine = lax.axis_index("samp")
    cols, dofs = r.shape
    recy = cn.shape[0] // 2
    rows_per = recy // n_samp
    quarters = 16 // rows_per
    wide = dofs // quarters // LANES
    pairs = dofs // PAIR
    low_half = lax.broadcasted_iota(jnp.int32, (cols, LANES), 1) < LANES // 2
    highest = lax.Precision.HIGHEST

    loads = [
        pltpu.make_async_copy(src, dst, in_sems.at[i])
        for i, (src, dst) in enumerate(
            (
                (c_in, uc_loc.at[0]),
                (sizes_in, sizes),
                (resid, r),
                (send_in, send_list),
                (u_in, uc_loc.at[1]),
                (diag, dg),
                (pattern_in, pattern),
                (stiff, st),
            )
        )
    ]
    for load in loads:
        load.start()

    barrier = pltpu.get_barrier_semaphore()
    chips = n_mesh // 2
    chip, core = lax.div(me, 2), lax.rem(me, 2)

    side = SQUARE
    row, column = lax.div(mine, side), lax.rem(mine, side)
    ring = [min(k, side - k) for k in range(side)]
    hops = sorted(range(1, n_samp), key=lambda o: -(ring[o // side] + ring[o % side]))
    peers = [side * lax.rem(row + o // side, side) + lax.rem(column + o % side, side) for o in hops]

    def greet(**device):
        pl.semaphore_signal(barrier, inc=1, device_id=device, device_id_type=MESH)

    for away in range(REACH, 0, -1):
        for by in (away, chips - away):
            for which in range(2):
                greet(mesh=2 * lax.rem(chip + by, chips) + which)
        if away == REACH:
            for peer in peers:
                greet(samp=peer)
    greet(mesh=2 * chip + 1 - core)

    def row_alive(start, width):
        live = sizes[0] * BLK
        return (lax.broadcasted_iota(jnp.int32, (1, width), 1) + start) < live

    def pack_panel(which):
        local = uc_loc[which].astype(F32)
        for q in range(quarters):
            for t in range(wide):
                at = (q * wide + t) * LANES
                stage[which, t, pl.ds(q, rows_per, stride=quarters), :] = local[:, at : at + LANES]
        packed = stage[which].astype(BF16)
        panel_send[which] = packed
        panel_got[which, mine] = packed

    def send_panel(which):
        for peer in peers:
            pltpu.make_async_remote_copy(
                src_ref=panel_send.at[which],
                dst_ref=panel_got.at[which, mine],
                send_sem=panel_ssem.at[which],
                recv_sem=panel_rsem.at[which],
                device_id={"samp": peer},
                device_id_type=MESH,
            ).start()

    def wait_panel(which, sems):
        others = panel_got.at[which, pl.ds(0, n_samp - 1)]
        pltpu.make_async_copy(others, others, sems.at[which]).wait()

    def natural(which, out):
        for k in range(n_samp):
            for t in range(wide):
                spread[t, 16 * k : 16 * k + 16, :] = panel_got[which, k, t].astype(F32)
        for q in range(quarters):
            for t in range(wide):
                at = (q * wide + t) * LANES
                tile = spread[t, pl.ds(q, recy, stride=quarters), :]
                tile = jnp.where(row_alive(at, LANES), tile, 0.0).astype(BF16)
                out[:recy, at : at + LANES] = tile
                out[recy:, at : at + LANES] = tile

    span = chips // 2
    part = lax.rem(chip, span)
    reducer = core == lax.rem(part, 2)
    own_sum = lax.div(chip, span) * TILES + part
    all_sums = 2 * TILES

    def rs_send(which, value):
        for t in range(TILES):
            pay[which, t] = value[8 * t : 8 * t + 8, :]

        def one(t, carry):
            away = lax.rem(chip - t + chips + span // 2 - 1, chips)
            slot = 2 * lax.rem(away, span) + core
            target = 2 * lax.rem(t + span * lax.div(away, span), chips) + lax.rem(t, 2)

            @pl.when(target != me)
            def _():
                pltpu.make_async_remote_copy(
                    src_ref=pay.at[which, t],
                    dst_ref=rs_got.at[which, slot],
                    send_sem=rs_ssem.at[which],
                    recv_sem=rs_rsem.at[which],
                    device_id={"mesh": target},
                    device_id_type=MESH,
                ).start()

            @pl.when(target == me)
            def _():
                rs_got[which, slot] = pay[which, t]

            return carry

        lax.fori_loop(0, TILES, one, 0)

    def tiles_done(sem, count):
        some = ar_got.at[pl.ds(0, count)]
        pltpu.make_async_copy(some, some, sem).wait()

    def ag_send(which):
        @pl.when(reducer)
        def _():
            tiles_done(rs_rsem.at[which], 2 * span - 1)
            total = rs_got[which, 0]
            for d in range(1, 2 * span):
                total = total + rs_got[which, d]
            at = which * all_sums + own_sum
            ar_got[at] = total

            def one(o, carry):
                half = lax.div(o + 1, 2)
                ahead = n_mesh // 2 + half * (1 - 2 * lax.rem(o, 2))
                pltpu.make_async_remote_copy(
                    src_ref=ar_got.at[at],
                    dst_ref=ar_got.at[at],
                    send_sem=ag_ssem.at[which],
                    recv_sem=ag_rsem.at[which],
                    device_id={"mesh": lax.rem(me + ahead, n_mesh)},
                    device_id_type=MESH,
                ).start()
                return carry

            lax.fori_loop(0, n_mesh - 1, one, 0)

    def ar_wait(which):
        @pl.when(reducer)
        def _():
            tiles_done(ag_rsem.at[which], all_sums - 1)

        @pl.when(jnp.logical_not(reducer))
        def _():
            tiles_done(ag_rsem.at[which], all_sums)

        at = which * all_sums
        return jnp.concatenate([ar_got[at + t] + ar_got[at + TILES + t] for t in range(TILES)], 0)

    def ar_sent(which):
        @pl.when(reducer)
        def _():
            tiles_done(rs_ssem.at[which], TILES - 1)
            tiles_done(ag_ssem.at[which], n_mesh - 1)

        @pl.when(jnp.logical_not(reducer))
        def _():
            tiles_done(rs_ssem.at[which], TILES)

    def fill_tables(m, row, tiles):
        n0, n1, n2 = tiles
        b0, b1, b2 = n0.astype(BF16), n1.astype(BF16), n2.astype(BF16)
        v0, v1, v2 = turned(n0).astype(BF16), turned(n1).astype(BF16), turned(n2).astype(BF16)
        even, odd, rows = 2 * m, 2 * m + 1, slice(row, row + cols)
        t0[even, rows] = b0
        r0t[even, rows] = v0
        t1[even, rows] = jnp.where(low_half, b1, v1)
        t0[odd, rows] = jnp.where(low_half, v1, v2)
        r0t[odd, rows] = jnp.where(low_half, b2, b1)
        t1[odd, rows] = jnp.where(low_half, v2, b2)

    def fill_split(source):
        def one(m, carry):
            at = pl.multiple_of(m * PAIR, PAIR)
            tiles = [source[:, pl.ds(at + j * LANES, LANES)] for j in range(3)]
            fill_tables(m, 0, tiles)
            fill_tables(m, cols, [x - x.astype(BF16).astype(F32) for x in tiles])
            return carry

        lax.fori_loop(0, pairs, one, 0, unroll=2)

    def ghost_copies(send, got, which):
        out = []
        for side, by in ((0, 1), (1, n_mesh - 1)):
            out.append(
                pltpu.make_async_remote_copy(
                    src_ref=send.at[side],
                    dst_ref=got.at[side],
                    send_sem=ghost_ssem.at[which, side],
                    recv_sem=ghost_rsem.at[which, side],
                    device_id={"mesh": lax.rem(me + by, n_mesh)},
                    device_id_type=MESH,
                )
            )
        return out

    def pack_ghosts(send, row, rows, copies=()):
        ends = (me == n_mesh - 1, me == 0)
        for side in range(2):
            keep = jnp.where(ends[side], 0.0, 1.0).astype(BF16)
            for start in range(0, rows, cols):
                span, to = slice(row + start, row + start + cols), slice(start, start + cols)
                for pair in range(GHOST // 2):
                    x, y = send_list[side, 2 * pair], send_list[side, 2 * pair + 1]
                    send[side, 2 * pair, to] = t0[x, span] * keep
                    send[side, 2 * pair + 1, to] = t0[y, span] * keep
                    send[side, GHOST + pair, to] = jnp.where(low_half, t1[x, span], t1[y, span]) * keep
            if copies:
                copies[side].start()

    def take_ghosts(got, row, rows):
        for side in range(2):
            base = 2 * pairs + side * GHOST
            for start in range(0, rows, cols):
                span, to = slice(start, start + cols), slice(row + start, row + start + cols)
                for pair in range(GHOST // 2):
                    for j in range(2):
                        x = got[side, 2 * pair + j, span]
                        t0[base + 2 * pair + j, to] = x
                        r0t[base + 2 * pair + j, to] = turned(x.astype(F32)).astype(BF16)
                    x = got[side, GHOST + pair, span]
                    y = turned(x.astype(F32)).astype(BF16)
                    t1[base + 2 * pair, to] = jnp.where(low_half, x, y)
                    t1[base + 2 * pair + 1, to] = jnp.where(low_half, y, x)

    def by_pairs(rows, low_rows, lanes, left, emit):
        def one(m, carry):
            at = pl.multiple_of(m * PAIR, PAIR)
            out0 = nt(left(2 * m), st[pl.ds(at, 2 * LANES), lanes])
            out1 = nt(left(2 * m + 1), st[pl.ds(at + LANES, 2 * LANES), lanes])
            emit(at, 0, out0[:, :LANES])
            emit(at, 1, jnp.where(low_rows, out0[:, LANES:], out1[:, :LANES]))
            emit(at, 2, out1[:, LANES:])
            return carry

        lax.fori_loop(0, pairs, one, 0, unroll=4)

    def apply_own(rows):
        low_rows = lax.broadcasted_iota(jnp.int32, (rows, LANES), 1) < LANES // 2
        none = jnp.zeros((rows, LANES), BF16)

        def left(i):
            return jnp.concatenate([t0[i, :rows], jnp.where(low_rows, t1[i, :rows], none)], 1)

        def emit(at, j, value):
            own[:rows, pl.ds(at + j * LANES, LANES)] = value

        by_pairs(rows, low_rows, slice(0, 2 * LANES), left, emit)

    def apply_stiff(rows, emit):
        low_rows = lax.broadcasted_iota(jnp.int32, (rows, LANES), 1) < LANES // 2
        none = jnp.zeros((rows, LANES), BF16)

        def left(i):
            parts = []
            for s in range(0, SLOTS, 2):
                x, y = pattern[s, i], pattern[s + 1, i]
                turned_y = r0t[y, :rows]
                if s:
                    parts.append(t0[x, :rows])
                parts.append(jnp.where(low_rows, t1[x, :rows] if s else none, turned_y))
                parts.append(jnp.where(low_rows, turned_y, t1[y, :rows]))
            return jnp.concatenate(parts, 1)

        def whole(at, j, value):
            emit(at, j, value + own[:rows, pl.ds(at + j * LANES, LANES)])

        by_pairs(rows, low_rows, slice(LANES, SLOTS * BLK), left, whole)

    def emit_first(at, j, value):
        span = pl.ds(at + j * LANES, LANES)
        keep, scale = row_alive(at + j * LANES, LANES), dg[:, span]
        a[:, span] = jnp.where(keep, halves(value[: 2 * cols]) + scale * r[:, span], 0.0)
        image = value[2 * cols :] + scale * cn[:recy, span].astype(F32)
        image = jnp.where(keep, image, 0.0).astype(BF16)
        dn[:recy, span] = image
        dn[recy:, span] = image

    def emit_second(at, j, value):
        span = pl.ds(at + j * LANES, LANES)
        b[:, span] = jnp.where(
            row_alive(at + j * LANES, LANES), halves(value) + dg[:, span] * a[:, span], 0.0
        )

    def renew(make, r_to, w_to):
        def one(m, carry):
            ww, wr = carry
            at = pl.multiple_of(m * PAIR, PAIR)
            span = pl.ds(at, PAIR)
            new_r, image = make(span)
            r_to[:, span] = new_r
            w_to[:, span] = image
            high = image.astype(BF16)
            wb[:cols, span] = high
            wb[cols:, span] = (image - high.astype(F32)).astype(BF16)
            for j in range(3):
                x = image[:, j * LANES : (j + 1) * LANES]
                ww = ww + x * x
                wr = wr + x * new_r[:, j * LANES : (j + 1) * LANES]
            return ww, wr

        zero = jnp.zeros((cols, LANES), F32)
        ww, wr = lax.fori_loop(0, pairs, one, (zero, zero), unroll=4)
        proj = halves(nt(wb[...], cn[:recy]))
        ww = jnp.sum(ww, axis=1, keepdims=True)
        wr = jnp.sum(wr, axis=1, keepdims=True)
        lane = lax.broadcasted_iota(jnp.int32, (cols, LANES - recy), 1)
        return jnp.concatenate([proj, jnp.where(lane == 0, ww, jnp.where(lane == 1, wr, 0.0))], 1)

    def step_of(reduced, c_r):
        proj = reduced[:, :recy]
        ww = reduced[:, recy : recy + 1]
        wr = reduced[:, recy + 1 : recy + 2]
        p_gram = jnp.dot(proj, gram, precision=highest, preferred_element_type=F32)
        bottom = ww + jnp.sum(proj * (p_gram - 2.0 * proj), axis=1, keepdims=True)
        top = wr - jnp.sum(proj * c_r, axis=1, keepdims=True)
        step = top / bottom
        return proj, step, c_r - step * (proj - p_gram)

    loads[0].wait()
    pack_panel(0)
    pl.semaphore_wait(barrier, 4 * REACH + n_samp)
    for by in (REACH, chips - REACH):
        peer = 2 * lax.rem(chip + by, chips) + core
        pl.semaphore_signal(far_sem, inc=1, device_id={"mesh": peer}, device_id_type=MESH)
    send_panel(0)
    loads[1].wait()
    loads[2].wait()

    def mask(m, carry):
        at = pl.multiple_of(m * PAIR, PAIR)
        span = pl.ds(at, PAIR)
        kept = jnp.where(row_alive(at, PAIR), r[:, span], 0.0)
        r[:, span] = kept
        rb[:, span] = kept.astype(BF16)
        return carry

    lax.fori_loop(0, pairs, mask, 0)
    fill_split(r)
    loads[3].wait()
    pack_ghosts(send_f.at[0], 0, 2 * cols, ghost_copies(send_f.at[0], got_f.at[0], 0))
    loads[4].wait()
    pack_panel(1)
    wait_panel(0, panel_rsem)
    natural(0, cn)
    first = nt(jnp.concatenate([rb[...], cn[:recy]], 0), cn[:recy])
    rs_send(0, jnp.concatenate([first[:cols], first[cols:]], 1))

    send_panel(1)
    def fill_panel(m, carry):
        at = pl.multiple_of(m * PAIR, PAIR)
        fill_tables(m, 2 * cols, [cn[:recy, pl.ds(at + j * LANES, LANES)].astype(F32) for j in range(3)])
        return carry

    lax.fori_loop(0, pairs, fill_panel, 0, unroll=2)
    pack_ghosts(send_c, 2 * cols, recy, ghost_copies(send_c, got_c, 1))
    for copy in ghost_copies(send_f.at[0], got_f.at[0], 0):
        copy.wait()
    take_ghosts(got_f.at[0], 0, 2 * cols)
    for load in loads[5:]:
        load.wait()
    apply_own(2 * cols + recy)
    pl.semaphore_wait(far_sem, 2)
    ag_send(0)
    for copy in ghost_copies(send_c, got_c, 1):
        copy.wait()
    take_ghosts(got_c, 2 * cols, recy)
    apply_stiff(2 * cols + recy, emit_first)
    reduced = ar_wait(0)
    coef = reduced[:, :recy]
    gram = reduced[:, recy:]
    coef2 = split2(coef)

    def make_first(span):
        new_r = r[:, span] - nn(coef2, cn[:, span])
        return new_r, a[:, span] - nn(coef2, dn[:, span])

    rs_send(1, renew(make_first, r, a))

    coef_t[...] = coef.T
    c_r = coef - jnp.dot(coef, gram, precision=highest, preferred_element_type=F32)
    fill_split(a)
    pack_ghosts(send_f.at[1], 0, 2 * cols, ghost_copies(send_f.at[1], got_f.at[1], 2))
    apply_own(2 * cols)
    wait_panel(1, panel_rsem)
    natural(1, un)
    ag_send(1)
    for copy in ghost_copies(send_f.at[1], got_f.at[1], 2):
        copy.wait()
    take_ghosts(got_f.at[1], 0, 2 * cols)
    apply_stiff(2 * cols, emit_second)
    proj, step1, c_r = step_of(ar_wait(1), c_r)
    proj2 = split2(proj)

    def make_second(span):
        image = a[:, span]
        new_r = r[:, span] - step1 * (image - nn(proj2, cn[:, span]))
        return new_r, image - step1 * (b[:, span] - nn(proj2, dn[:, span]))

    rs_send(2, renew(make_second, r_next, w_next))

    carried2 = split2(coef - step1 * proj)

    def base(m, carry):
        span = pl.ds(pl.multiple_of(m * PAIR, PAIR), PAIR)
        rounded = r[:, span].astype(BF16).astype(F32)
        base_sol[:, span] = nn(carried2, un[:, span]) + step1 * rounded
        return carry

    lax.fori_loop(0, pairs, base, 0, unroll=2)
    outs = [
        pltpu.make_async_copy(src, dst, out_sems.at[i])
        for i, (src, dst) in enumerate(
            (
                (r_next, fields_out.at[0]),
                (w_next, fields_out.at[1]),
                (base_sol, fields_out.at[2]),
                (cn.at[:recy], panels_out.at[0]),
                (un.at[:recy], panels_out.at[1]),
                (coef_t, coef_out),
                (fin, fin_out),
            )
        )
    ]
    for copy in outs[:6]:
        copy.start()
    for which in range(2):
        wait_panel(which, panel_ssem)
        ar_sent(which)
    ag_send(2)
    proj, step2, _ = step_of(ar_wait(2), c_r)
    fin[...] = jnp.concatenate([proj, jnp.broadcast_to(step2, (cols, LANES - recy))], 1)
    outs[6].start()
    ar_sent(2)
    for copy in outs:
        copy.wait()

def last_kernel(
    fields_in, panels_in, fin_in, coef_in,
    sol_out, res_out, coef_out,
    fields, panels, fin, in_sems, out_sems,
):
    _, cols, dofs = fields.shape
    recy = panels.shape[1]
    width = dofs // PARTS
    fin_copy = pltpu.make_async_copy(fin_in, fin, out_sems.at[0, 1])
    fin_copy.start()
    loads, outs = [], []
    for i in range(PARTS):
        span = pl.ds(i * width, width)
        loads.append(
            [
                pltpu.make_async_copy(src.at[:, :, span], dst.at[:, :, span], in_sems.at[i, j])
                for j, (src, dst) in enumerate(((panels_in, panels), (fields_in, fields)))
            ]
        )
        for load in loads[-1]:
            load.start()
    coef_copy = pltpu.make_async_copy(coef_in, coef_out, out_sems.at[0, 0])
    coef_copy.start()
    fin_copy.wait()
    proj, step = fin[:, :recy], fin[:, recy : recy + 1]
    high = proj.astype(BF16)
    proj2 = jnp.concatenate([high, (proj - high.astype(F32)).astype(BF16)], 0)
    for i in range(PARTS):
        for load in loads[i]:
            load.wait()
        at = slice(i * width, (i + 1) * width)
        old = fields[0, :, at]
        fields[0, :, at] = old - step * (fields[1, :, at] - halves(nn(proj2, panels[0, :, at])))
        rounded = old.astype(BF16).astype(F32)
        fields[2, :, at] = fields[2, :, at] + step * (rounded - halves(nn(proj2, panels[1, :, at])))
        for j, dst in ((0, res_out), (2, sol_out)):
            span = pl.ds(i * width, width)
            out = pltpu.make_async_copy(fields.at[j, :, span], dst.at[:, span], out_sems.at[i + 1, j // 2])
            out.start()
            outs.append(out)
    coef_copy.wait()
    for out in outs:
        out.wait()


def per_device(resid_in, recycle_u, recycle_c, stiff, diag_scale, pattern, send_list, part_sizes, n_mesh, n_samp):
    cols, dofs = resid_in.shape
    blocks, blk, width = stiff.shape
    recy = recycle_c.shape[0] * n_samp
    wide = dofs * recycle_c.shape[0] // 16 // LANES
    ext = blocks + 2 * GHOST
    hbm = pl.BlockSpec(memory_space=pltpu.HBM)
    dma = pltpu.SemaphoreType.DMA
    field = pltpu.VMEM((cols, dofs), F32)
    panel = pltpu.VMEM((2 * recy, dofs), BF16)
    table = pltpu.VMEM((ext, 2 * cols + recy, LANES), BF16)
    middle = pl.pallas_call(
        functools.partial(kernel, n_mesh, n_samp),
        out_shape=(
            jax.ShapeDtypeStruct((3, cols, dofs), F32),
            jax.ShapeDtypeStruct((2, recy, dofs), BF16),
            jax.ShapeDtypeStruct((cols, LANES), F32),
            jax.ShapeDtypeStruct((recy, cols), F32),
        ),
        in_specs=[hbm] * 8,
        out_specs=(hbm,) * 4,
        scratch_shapes=[
            field,
            field,
            field,
            field,
            field,
            field,
            pltpu.VMEM((cols, LANES), F32),
            pltpu.VMEM((recy, cols), F32),
            pltpu.VMEM((2 * cols + recy, dofs), F32),
            pltpu.VMEM((2, recycle_c.shape[0], dofs), BF16),
            pltpu.VMEM((blocks * blk, width), BF16),
            pltpu.VMEM((1, dofs), F32),
            pltpu.SMEM(pattern.shape[::-1], jnp.int32),
            pltpu.SMEM(send_list.shape, jnp.int32),
            pltpu.SMEM(part_sizes.shape, jnp.int32),
            pltpu.VMEM((2, wide, 16, LANES), F32),
            pltpu.VMEM((2, wide, 16, LANES), BF16),
            pltpu.VMEM((2, n_samp, wide, 16, LANES), BF16),
            pltpu.VMEM((wide, 16 * n_samp, LANES), F32),
            panel,
            panel,
            panel,
            pltpu.VMEM((cols, dofs), BF16),
            pltpu.VMEM((2 * cols, dofs), BF16),
            table,
            table,
            table,
            pltpu.VMEM((ITERS, 2, GHOST + GHOST // 2, 2 * cols, LANES), BF16),
            pltpu.VMEM((ITERS, 2, GHOST + GHOST // 2, 2 * cols, LANES), BF16),
            pltpu.VMEM((2, GHOST + GHOST // 2, recy, LANES), BF16),
            pltpu.VMEM((2, GHOST + GHOST // 2, recy, LANES), BF16),
            pltpu.VMEM((ITERS + 1, TILES, 8, LANES), F32),
            pltpu.VMEM((ITERS + 1, n_mesh // 2, 8, LANES), F32),
            pltpu.VMEM(((ITERS + 1) * 2 * TILES, 8, LANES), F32),
            dma((8,)),
            dma((2,)),
            dma((2,)),
            dma((ITERS + 1, 2)),
            dma((ITERS + 1, 2)),
            dma((ITERS + 1,)),
            dma((ITERS + 1,)),
            dma((ITERS + 1,)),
            dma((ITERS + 1,)),
            dma((7,)),
            pltpu.SemaphoreType.REGULAR,
        ],
        compiler_params=pltpu.CompilerParams(
            collective_id=0, has_side_effects=True, vmem_limit_bytes=62 << 20
        ),
    )(
        resid_in,
        recycle_u,
        recycle_c,
        stiff.reshape(blocks * blk, width),
        diag_scale.reshape(1, dofs),
        pattern.T,
        send_list,
        part_sizes,
    )
    return pl.pallas_call(
        last_kernel,
        out_shape=(
            jax.ShapeDtypeStruct((cols, dofs), F32),
            jax.ShapeDtypeStruct((cols, dofs), F32),
            jax.ShapeDtypeStruct((recy, cols), F32),
        ),
        in_specs=[hbm] * 4,
        out_specs=(hbm,) * 3,
        scratch_shapes=[
            pltpu.VMEM((3, cols, dofs), F32),
            pltpu.VMEM((2, recy, dofs), BF16),
            pltpu.VMEM((cols, LANES), F32),
            dma((PARTS, 2)),
            dma((PARTS + 1, 2)),
        ],
        compiler_params=pltpu.CompilerParams(vmem_limit_bytes=62 << 20),
    )(*middle)


def solution(mesh):
    body = functools.partial(per_device, n_mesh=mesh.shape["mesh"], n_samp=mesh.shape["samp"])
    return jax.shard_map(
        body,
        mesh=mesh,
        in_specs=(
            P("samp", "mesh"),
            P("samp", "mesh"),
            P("samp", "mesh"),
            P("mesh", None, None),
            P("mesh"),
            P("mesh", None),
            P("mesh", None),
            P("mesh"),
        ),
        out_specs=(P("samp", "mesh"), P("samp", "mesh"), P(None, "samp")),
        check_vma=False,
    )
```

```python
import functools

import jax
import jax.numpy as jnp
from jax import lax
from jax.experimental import pallas as pl
from jax.experimental.pallas import tpu as pltpu
from jax.sharding import PartitionSpec as P

MESH = pl.DeviceIdType.MESH
F32 = jnp.float32
BF16 = jnp.bfloat16
LANES = 128
BLK = 192
PAIR = 2 * BLK
SLOTS = 6
GHOST = 8
ITERS = 2
TILES = 8
REACH = 4
SQUARE = 4
PARTS = 2


def nt(a, b):
    return lax.dot_general(a, b, (((1,), (1,)), ((), ())), preferred_element_type=F32)


def nn(a, b):
    return lax.dot_general(a, b, (((1,), (0,)), ((), ())), preferred_element_type=F32)


def split2(x):
    high = x.astype(BF16).astype(F32)
    return jnp.concatenate([high, x - high], 1).astype(BF16)


def halves(x):
    rows = x.shape[0] // 2
    return x[:rows] + x[rows:]


def turned(x):
    return pltpu.roll(x, LANES // 2, 1)


def kernel(
    n_mesh, n_samp,
    resid, u_in, c_in, stiff, diag, pattern_in, send_in, sizes_in,
    fields_out, panels_out, fin_out, coef_out,
    r, a, b, r_next, w_next, base_sol, fin, coef_t, own,
    uc_loc, st, dg, pattern, send_list, sizes,
    stage, panel_send, panel_got, spread, cn, un, dn, rb, wb,
    t0, t1, r0t, send_f, got_f, send_c, got_c,
    pay, rs_got, ar_got,
    in_sems, panel_ssem, panel_rsem, ghost_ssem, ghost_rsem, rs_ssem, rs_rsem, ag_ssem, ag_rsem, out_sems, far_sem,
):
    me = lax.axis_index("mesh")
    mine = lax.axis_index("samp")
    cols, dofs = r.shape
    recy = cn.shape[0] // 2
    rows_per = recy // n_samp
    quarters = 16 // rows_per
    wide = dofs // quarters // LANES
    pairs = dofs // PAIR
    low_half = lax.broadcasted_iota(jnp.int32, (cols, LANES), 1) < LANES // 2

    loads = [
        pltpu.make_async_copy(src, dst, in_sems.at[i])
        for i, (src, dst) in enumerate(
            (
                (c_in, uc_loc.at[0]),
                (sizes_in, sizes),
                (resid, r),
                (send_in, send_list),
                (u_in, uc_loc.at[1]),
                (diag, dg),
                (pattern_in, pattern),
                (stiff, st),
            )
        )
    ]
    for load in loads:
        load.start()

    barrier = pltpu.get_barrier_semaphore()
    chips = n_mesh // 2
    chip, core = lax.div(me, 2), lax.rem(me, 2)

    side = SQUARE
    row, column = lax.div(mine, side), lax.rem(mine, side)
    ring = [min(k, side - k) for k in range(side)]
    hops = sorted(range(1, n_samp), key=lambda o: -(ring[o // side] + ring[o % side]))
    peers = [side * lax.rem(row + o // side, side) + lax.rem(column + o % side, side) for o in hops]

    def greet(**device):
        pl.semaphore_signal(barrier, inc=1, device_id=device, device_id_type=MESH)

    for away in range(REACH, 0, -1):
        for by in (away, chips - away):
            for which in range(2):
                greet(mesh=2 * lax.rem(chip + by, chips) + which)
        if away == REACH:
            for peer in peers:
                greet(samp=peer)
    greet(mesh=2 * chip + 1 - core)

    def row_alive(start, width):
        live = sizes[0] * BLK
        return (lax.broadcasted_iota(jnp.int32, (1, width), 1) + start) < live

    def pack_panel(which):
        local = uc_loc[which].astype(F32)
        for q in range(quarters):
            for t in range(wide):
                at = (q * wide + t) * LANES
                stage[which, t, pl.ds(q, rows_per, stride=quarters), :] = local[:, at : at + LANES]
        packed = stage[which].astype(BF16)
        panel_send[which] = packed
        panel_got[which, mine] = packed

    def send_panel(which):
        for peer in peers:
            pltpu.make_async_remote_copy(
                src_ref=panel_send.at[which],
                dst_ref=panel_got.at[which, mine],
                send_sem=panel_ssem.at[which],
                recv_sem=panel_rsem.at[which],
                device_id={"samp": peer},
                device_id_type=MESH,
            ).start()

    def wait_panel(which, sems):
        others = panel_got.at[which, pl.ds(0, n_samp - 1)]
        pltpu.make_async_copy(others, others, sems.at[which]).wait()

    def natural(which, out):
        for k in range(n_samp):
            for t in range(wide):
                spread[t, 16 * k : 16 * k + 16, :] = panel_got[which, k, t].astype(F32)
        for q in range(quarters):
            for t in range(wide):
                at = (q * wide + t) * LANES
                tile = spread[t, pl.ds(q, recy, stride=quarters), :]
                tile = jnp.where(row_alive(at, LANES), tile, 0.0).astype(BF16)
                out[:recy, at : at + LANES] = tile
                out[recy:, at : at + LANES] = tile

    span = chips // 2
    back = span // 2 - 1
    part = lax.rem(chip, span)
    reducer = core == lax.rem(part, 2)
    own_sum = lax.div(chip, span) * TILES + part
    all_sums = 2 * TILES

    rows_packed = cols // 2 // TILES
    eye = lax.broadcasted_iota(jnp.int32, (cols, cols), 0) == lax.broadcasted_iota(jnp.int32, (cols, cols), 1)

    def as_row(column):
        return jnp.sum(jnp.where(eye, column, 0.0), axis=0, keepdims=True)

    def as_column(row):
        return jnp.sum(jnp.where(eye, row, 0.0), axis=1, keepdims=True)

    def rs_send(which, value, extra):
        packed = jnp.concatenate([value[: cols // 2], value[cols // 2 :]], 1)
        for t in range(TILES):
            pay[which, t, :rows_packed] = packed[rows_packed * t : rows_packed * (t + 1), :]
            pay[which, t, rows_packed:] = extra

        for ahead in sorted(range(span), key=lambda k: -abs(k - back)):
            t = lax.rem(chip + back - ahead + chips, span)
            slot = 2 * ahead + core
            near = lax.rem(chip + back - ahead + chips, chips)
            target = 2 * near + lax.rem(t, 2)

            @pl.when(target != me)
            def _():
                pltpu.make_async_remote_copy(
                    src_ref=pay.at[which, t],
                    dst_ref=rs_got.at[which, slot],
                    send_sem=rs_ssem.at[which],
                    recv_sem=rs_rsem.at[which],
                    device_id={"mesh": target},
                    device_id_type=MESH,
                ).start()

            @pl.when(target == me)
            def _():
                rs_got[which, slot] = pay[which, t]

    def tiles_done(sem, count):
        some = ar_got.at[pl.ds(0, count)]
        pltpu.make_async_copy(some, some, sem).wait()

    def ag_send(which):
        @pl.when(reducer)
        def _():
            tiles_done(rs_rsem.at[which], 2 * span - 1)
            total = rs_got[which, 0]
            for d in range(1, 2 * span):
                total = total + rs_got[which, d]
            at = which * all_sums + own_sum
            ar_got[at] = total

            half = n_mesh // 2
            for ahead in sorted(range(1, n_mesh), key=lambda k: abs(k - half)):
                pltpu.make_async_remote_copy(
                    src_ref=ar_got.at[at],
                    dst_ref=ar_got.at[at],
                    send_sem=ag_ssem.at[which],
                    recv_sem=ag_rsem.at[which],
                    device_id={"mesh": lax.rem(me + ahead, n_mesh)},
                    device_id_type=MESH,
                ).start()

    def ar_wait(which):
        @pl.when(reducer)
        def _():
            tiles_done(ag_rsem.at[which], all_sums - 1)

        @pl.when(jnp.logical_not(reducer))
        def _():
            tiles_done(ag_rsem.at[which], all_sums)

        at = which * all_sums
        tiles = [ar_got[at + t] + ar_got[at + TILES + t] for t in range(TILES)]
        packed = jnp.concatenate([tile[:rows_packed] for tile in tiles], 0)
        value = jnp.concatenate([packed[:, :recy], packed[:, recy:]], 0)
        return value, tiles[0][rows_packed:]

    def ar_sent(which):
        @pl.when(reducer)
        def _():
            tiles_done(rs_ssem.at[which], TILES - 1)
            tiles_done(ag_ssem.at[which], n_mesh - 1)

        @pl.when(jnp.logical_not(reducer))
        def _():
            tiles_done(rs_ssem.at[which], TILES)

    def fill_tables(m, row, tiles):
        n0, n1, n2 = tiles
        b0, b1, b2 = n0.astype(BF16), n1.astype(BF16), n2.astype(BF16)
        v0, v1, v2 = turned(n0).astype(BF16), turned(n1).astype(BF16), turned(n2).astype(BF16)
        even, odd, rows = 2 * m, 2 * m + 1, slice(row, row + cols)
        t0[even, rows] = b0
        r0t[even, rows] = v0
        t1[even, rows] = jnp.where(low_half, b1, v1)
        t0[odd, rows] = jnp.where(low_half, v1, v2)
        r0t[odd, rows] = jnp.where(low_half, b2, b1)
        t1[odd, rows] = jnp.where(low_half, v2, b2)

    def fill_split(source):
        def one(m, carry):
            at = pl.multiple_of(m * PAIR, PAIR)
            tiles = [source[:, pl.ds(at + j * LANES, LANES)] for j in range(3)]
            fill_tables(m, 0, tiles)
            fill_tables(m, cols, [x - x.astype(BF16).astype(F32) for x in tiles])
            return carry

        lax.fori_loop(0, pairs, one, 0, unroll=2)

    def ghost_copies(send, got, which):
        out = []
        for side, by in ((0, 1), (1, n_mesh - 1)):
            out.append(
                pltpu.make_async_remote_copy(
                    src_ref=send.at[side],
                    dst_ref=got.at[side],
                    send_sem=ghost_ssem.at[which, side],
                    recv_sem=ghost_rsem.at[which, side],
                    device_id={"mesh": lax.rem(me + by, n_mesh)},
                    device_id_type=MESH,
                )
            )
        return out

    def pack_ghosts(send, row, rows, copies=()):
        ends = (me == n_mesh - 1, me == 0)
        for side in range(2):
            keep = jnp.where(ends[side], 0.0, 1.0).astype(BF16)
            for start in range(0, rows, cols):
                span, to = slice(row + start, row + start + cols), slice(start, start + cols)
                for pair in range(GHOST // 2):
                    x, y = send_list[side, 2 * pair], send_list[side, 2 * pair + 1]
                    send[side, 2 * pair, to] = t0[x, span] * keep
                    send[side, 2 * pair + 1, to] = t0[y, span] * keep
                    send[side, GHOST + pair, to] = jnp.where(low_half, t1[x, span], t1[y, span]) * keep
            if copies:
                copies[side].start()

    def take_ghosts(got, row, rows):
        for side in range(2):
            base = 2 * pairs + side * GHOST
            for start in range(0, rows, cols):
                span, to = slice(start, start + cols), slice(row + start, row + start + cols)
                for pair in range(GHOST // 2):
                    for j in range(2):
                        x = got[side, 2 * pair + j, span]
                        t0[base + 2 * pair + j, to] = x
                        r0t[base + 2 * pair + j, to] = turned(x.astype(F32)).astype(BF16)
                    x = got[side, GHOST + pair, span]
                    y = turned(x.astype(F32)).astype(BF16)
                    t1[base + 2 * pair, to] = jnp.where(low_half, x, y)
                    t1[base + 2 * pair + 1, to] = jnp.where(low_half, y, x)

    def by_pairs(rows, low_rows, lanes, left, emit):
        def one(m, carry):
            at = pl.multiple_of(m * PAIR, PAIR)
            out0 = nt(left(2 * m), st[pl.ds(at, 2 * LANES), lanes])
            out1 = nt(left(2 * m + 1), st[pl.ds(at + LANES, 2 * LANES), lanes])
            emit(at, 0, out0[:, :LANES])
            emit(at, 1, jnp.where(low_rows, out0[:, LANES:], out1[:, :LANES]))
            emit(at, 2, out1[:, LANES:])
            return carry

        lax.fori_loop(0, pairs, one, 0, unroll=4)

    def apply_own(rows):
        low_rows = lax.broadcasted_iota(jnp.int32, (rows, LANES), 1) < LANES // 2
        none = jnp.zeros((rows, LANES), BF16)

        def left(i):
            return jnp.concatenate([t0[i, :rows], jnp.where(low_rows, t1[i, :rows], none)], 1)

        def emit(at, j, value):
            own[:rows, pl.ds(at + j * LANES, LANES)] = value

        by_pairs(rows, low_rows, slice(0, 2 * LANES), left, emit)

    def apply_stiff(rows, emit):
        low_rows = lax.broadcasted_iota(jnp.int32, (rows, LANES), 1) < LANES // 2
        none = jnp.zeros((rows, LANES), BF16)

        def left(i):
            parts = []
            for s in range(0, SLOTS, 2):
                x, y = pattern[s, i], pattern[s + 1, i]
                turned_y = r0t[y, :rows]
                if s:
                    parts.append(t0[x, :rows])
                parts.append(jnp.where(low_rows, t1[x, :rows] if s else none, turned_y))
                parts.append(jnp.where(low_rows, turned_y, t1[y, :rows]))
            return jnp.concatenate(parts, 1)

        def whole(at, j, value):
            emit(at, j, value + own[:rows, pl.ds(at + j * LANES, LANES)])

        by_pairs(rows, low_rows, slice(LANES, SLOTS * BLK), left, whole)

    def emit_first(at, j, value):
        span = pl.ds(at + j * LANES, LANES)
        keep, scale = row_alive(at + j * LANES, LANES), dg[:, span]
        a[:, span] = jnp.where(keep, halves(value[: 2 * cols]) + scale * r[:, span], 0.0)
        image = value[2 * cols :] + scale * cn[:recy, span].astype(F32)
        image = jnp.where(keep, image, 0.0).astype(BF16)
        dn[:recy, span] = image
        dn[recy:, span] = image

    def emit_second(at, j, value):
        span = pl.ds(at + j * LANES, LANES)
        b[:, span] = jnp.where(
            row_alive(at + j * LANES, LANES), halves(value) + dg[:, span] * a[:, span], 0.0
        )

    def renew(make, r_to, w_to):
        def one(m, carry):
            ww, wr = carry
            at = pl.multiple_of(m * PAIR, PAIR)
            span = pl.ds(at, PAIR)
            new_r, image = make(span)
            r_to[:, span] = new_r
            w_to[:, span] = image
            high = image.astype(BF16)
            wb[:cols, span] = high
            wb[cols:, span] = (image - high.astype(F32)).astype(BF16)
            for j in range(3):
                x = image[:, j * LANES : (j + 1) * LANES]
                ww = ww + x * x
                wr = wr + x * new_r[:, j * LANES : (j + 1) * LANES]
            return ww, wr

        zero = jnp.zeros((cols, LANES), F32)
        ww, wr = lax.fori_loop(0, pairs, one, (zero, zero), unroll=4)
        proj = halves(nt(wb[...], cn[:recy]))
        ww = jnp.sum(ww, axis=1, keepdims=True)
        wr = jnp.sum(wr, axis=1, keepdims=True)
        return proj, jnp.concatenate([as_row(ww), as_row(wr)], 1)

    def times_gram(x):
        high = x.astype(BF16).astype(F32)
        gram_high = gram.astype(BF16).astype(F32)
        left = jnp.concatenate([high, x - high, high], 1).astype(BF16)
        return nn(left, jnp.concatenate([gram_high, gram_high, gram - gram_high], 0).astype(BF16))

    def step_of(reduced, c_r):
        proj, extra = reduced
        ww, wr = as_column(extra[:, :cols]), as_column(extra[:, cols:])
        p_gram = times_gram(proj)
        bottom = ww + jnp.sum(proj * (p_gram - 2.0 * proj), axis=1, keepdims=True)
        top = wr - jnp.sum(proj * c_r, axis=1, keepdims=True)
        step = top / bottom
        return proj, step, c_r - step * (proj - p_gram)

    loads[0].wait()
    pack_panel(0)
    pl.semaphore_wait(barrier, 4 * REACH + n_samp)
    for by in (REACH, chips - REACH):
        peer = 2 * lax.rem(chip + by, chips) + core
        pl.semaphore_signal(far_sem, inc=1, device_id={"mesh": peer}, device_id_type=MESH)
    send_panel(0)
    loads[1].wait()
    loads[2].wait()

    def mask(m, carry):
        at = pl.multiple_of(m * PAIR, PAIR)
        span = pl.ds(at, PAIR)
        kept = jnp.where(row_alive(at, PAIR), r[:, span], 0.0)
        r[:, span] = kept
        rb[:, span] = kept.astype(BF16)
        return carry

    lax.fori_loop(0, pairs, mask, 0)
    fill_split(r)
    loads[3].wait()
    pack_ghosts(send_f.at[0], 0, 2 * cols, ghost_copies(send_f.at[0], got_f.at[0], 0))
    loads[4].wait()
    pack_panel(1)
    wait_panel(0, panel_rsem)
    natural(0, cn)
    first = nt(jnp.concatenate([rb[...], cn[:recy]], 0), cn[:recy])
    no_extra = jnp.zeros((1, LANES), F32)
    rs_send(0, first[:cols], no_extra)
    rs_send(ITERS + 1, first[cols:], no_extra)

    def fill_panel(m, carry):
        at = pl.multiple_of(m * PAIR, PAIR)
        fill_tables(m, 2 * cols, [cn[:recy, pl.ds(at + j * LANES, LANES)].astype(F32) for j in range(3)])
        return carry

    lax.fori_loop(0, pairs, fill_panel, 0, unroll=2)
    pack_ghosts(send_c, 2 * cols, recy, ghost_copies(send_c, got_c, 1))
    for copy in ghost_copies(send_f.at[0], got_f.at[0], 0):
        copy.wait()
    take_ghosts(got_f.at[0], 0, 2 * cols)
    for load in loads[5:]:
        load.wait()
    apply_own(2 * cols + recy)
    pl.semaphore_wait(far_sem, 2)
    ag_send(0)
    for copy in ghost_copies(send_c, got_c, 1):
        copy.wait()
    take_ghosts(got_c, 2 * cols, recy)
    apply_stiff(2 * cols + recy, emit_first)
    coef, _ = ar_wait(0)
    coef2 = split2(coef)

    def make_first(span):
        new_r = r[:, span] - nn(coef2, cn[:, span])
        return new_r, a[:, span] - nn(coef2, dn[:, span])

    rs_send(1, *renew(make_first, r, a))

    coef_t[...] = coef.T
    fill_split(a)
    pack_ghosts(send_f.at[1], 0, 2 * cols, ghost_copies(send_f.at[1], got_f.at[1], 2))
    ag_send(ITERS + 1)
    apply_own(2 * cols)
    ag_send(1)
    send_panel(1)
    for copy in ghost_copies(send_f.at[1], got_f.at[1], 2):
        copy.wait()
    take_ghosts(got_f.at[1], 0, 2 * cols)
    apply_stiff(2 * cols, emit_second)
    gram, _ = ar_wait(ITERS + 1)
    c_r = coef - times_gram(coef)
    proj, step1, c_r = step_of(ar_wait(1), c_r)
    proj2 = split2(proj)

    def make_second(span):
        image = a[:, span]
        new_r = r[:, span] - step1 * (image - nn(proj2, cn[:, span]))
        return new_r, image - step1 * (b[:, span] - nn(proj2, dn[:, span]))

    rs_send(2, *renew(make_second, r_next, w_next))

    wait_panel(1, panel_rsem)
    natural(1, un)
    carried2 = split2(coef - step1 * proj)

    def base(m, carry):
        span = pl.ds(pl.multiple_of(m * PAIR, PAIR), PAIR)
        rounded = r[:, span].astype(BF16).astype(F32)
        base_sol[:, span] = nn(carried2, un[:, span]) + step1 * rounded
        return carry

    lax.fori_loop(0, pairs, base, 0, unroll=2)
    outs = [
        pltpu.make_async_copy(src, dst, out_sems.at[i])
        for i, (src, dst) in enumerate(
            (
                (r_next, fields_out.at[0]),
                (w_next, fields_out.at[1]),
                (base_sol, fields_out.at[2]),
                (cn.at[:recy], panels_out.at[0]),
                (un.at[:recy], panels_out.at[1]),
                (coef_t, coef_out),
                (fin, fin_out),
            )
        )
    ]
    for copy in outs[:6]:
        copy.start()
    for which in range(2):
        wait_panel(which, panel_ssem)
        ar_sent(which)
    ar_sent(ITERS + 1)
    ag_send(2)
    proj, step2, _ = step_of(ar_wait(2), c_r)
    fin[...] = jnp.concatenate([proj, jnp.broadcast_to(step2, (cols, LANES - recy))], 1)
    outs[6].start()
    ar_sent(2)
    for copy in outs:
        copy.wait()

def last_kernel(
    fields_in, panels_in, fin_in, coef_in,
    sol_out, res_out, coef_out,
    fields, panels, fin, in_sems, out_sems,
):
    _, cols, dofs = fields.shape
    recy = panels.shape[1]
    width = dofs // PARTS
    fin_copy = pltpu.make_async_copy(fin_in, fin, out_sems.at[0, 1])
    fin_copy.start()
    loads, outs = [], []
    for i in range(PARTS):
        span = pl.ds(i * width, width)
        loads.append(
            [
                pltpu.make_async_copy(src.at[:, :, span], dst.at[:, :, span], in_sems.at[i, j])
                for j, (src, dst) in enumerate(((panels_in, panels), (fields_in, fields)))
            ]
        )
        for load in loads[-1]:
            load.start()
    coef_copy = pltpu.make_async_copy(coef_in, coef_out, out_sems.at[0, 0])
    coef_copy.start()
    fin_copy.wait()
    proj, step = fin[:, :recy], fin[:, recy : recy + 1]
    high = proj.astype(BF16)
    proj2 = jnp.concatenate([high, (proj - high.astype(F32)).astype(BF16)], 0)
    for i in range(PARTS):
        for load in loads[i]:
            load.wait()
        at = slice(i * width, (i + 1) * width)
        old = fields[0, :, at]
        fields[0, :, at] = old - step * (fields[1, :, at] - halves(nn(proj2, panels[0, :, at])))
        rounded = old.astype(BF16).astype(F32)
        fields[2, :, at] = fields[2, :, at] + step * (rounded - halves(nn(proj2, panels[1, :, at])))
        for j, dst in ((0, res_out), (2, sol_out)):
            span = pl.ds(i * width, width)
            out = pltpu.make_async_copy(fields.at[j, :, span], dst.at[:, span], out_sems.at[i + 1, j // 2])
            out.start()
            outs.append(out)
    coef_copy.wait()
    for out in outs:
        out.wait()


def per_device(resid_in, recycle_u, recycle_c, stiff, diag_scale, pattern, send_list, part_sizes, n_mesh, n_samp):
    cols, dofs = resid_in.shape
    blocks, blk, width = stiff.shape
    recy = recycle_c.shape[0] * n_samp
    wide = dofs * recycle_c.shape[0] // 16 // LANES
    ext = blocks + 2 * GHOST
    tile = cols // 2 // TILES + 1
    hbm = pl.BlockSpec(memory_space=pltpu.HBM)
    dma = pltpu.SemaphoreType.DMA
    field = pltpu.VMEM((cols, dofs), F32)
    panel = pltpu.VMEM((2 * recy, dofs), BF16)
    table = pltpu.VMEM((ext, 2 * cols + recy, LANES), BF16)
    middle = pl.pallas_call(
        functools.partial(kernel, n_mesh, n_samp),
        out_shape=(
            jax.ShapeDtypeStruct((3, cols, dofs), F32),
            jax.ShapeDtypeStruct((2, recy, dofs), BF16),
            jax.ShapeDtypeStruct((cols, LANES), F32),
            jax.ShapeDtypeStruct((recy, cols), F32),
        ),
        in_specs=[hbm] * 8,
        out_specs=(hbm,) * 4,
        scratch_shapes=[
            field,
            field,
            field,
            field,
            field,
            field,
            pltpu.VMEM((cols, LANES), F32),
            pltpu.VMEM((recy, cols), F32),
            pltpu.VMEM((2 * cols + recy, dofs), F32),
            pltpu.VMEM((2, recycle_c.shape[0], dofs), BF16),
            pltpu.VMEM((blocks * blk, width), BF16),
            pltpu.VMEM((1, dofs), F32),
            pltpu.SMEM(pattern.shape[::-1], jnp.int32),
            pltpu.SMEM(send_list.shape, jnp.int32),
            pltpu.SMEM(part_sizes.shape, jnp.int32),
            pltpu.VMEM((2, wide, 16, LANES), F32),
            pltpu.VMEM((2, wide, 16, LANES), BF16),
            pltpu.VMEM((2, n_samp, wide, 16, LANES), BF16),
            pltpu.VMEM((wide, 16 * n_samp, LANES), F32),
            panel,
            panel,
            panel,
            pltpu.VMEM((cols, dofs), BF16),
            pltpu.VMEM((2 * cols, dofs), BF16),
            table,
            table,
            table,
            pltpu.VMEM((ITERS, 2, GHOST + GHOST // 2, 2 * cols, LANES), BF16),
            pltpu.VMEM((ITERS, 2, GHOST + GHOST // 2, 2 * cols, LANES), BF16),
            pltpu.VMEM((2, GHOST + GHOST // 2, recy, LANES), BF16),
            pltpu.VMEM((2, GHOST + GHOST // 2, recy, LANES), BF16),
            pltpu.VMEM((ITERS + 2, TILES, tile, LANES), F32),
            pltpu.VMEM((ITERS + 2, n_mesh // 2, tile, LANES), F32),
            pltpu.VMEM(((ITERS + 2) * 2 * TILES, tile, LANES), F32),
            dma((8,)),
            dma((2,)),
            dma((2,)),
            dma((ITERS + 1, 2)),
            dma((ITERS + 1, 2)),
            dma((ITERS + 2,)),
            dma((ITERS + 2,)),
            dma((ITERS + 2,)),
            dma((ITERS + 2,)),
            dma((7,)),
            pltpu.SemaphoreType.REGULAR,
        ],
        compiler_params=pltpu.CompilerParams(
            collective_id=0, has_side_effects=True, vmem_limit_bytes=62 << 20
        ),
    )(
        resid_in,
        recycle_u,
        recycle_c,
        stiff.reshape(blocks * blk, width),
        diag_scale.reshape(1, dofs),
        pattern.T,
        send_list,
        part_sizes,
    )
    return pl.pallas_call(
        last_kernel,
        out_shape=(
            jax.ShapeDtypeStruct((cols, dofs), F32),
            jax.ShapeDtypeStruct((cols, dofs), F32),
            jax.ShapeDtypeStruct((recy, cols), F32),
        ),
        in_specs=[hbm] * 4,
        out_specs=(hbm,) * 3,
        scratch_shapes=[
            pltpu.VMEM((3, cols, dofs), F32),
            pltpu.VMEM((2, recy, dofs), BF16),
            pltpu.VMEM((cols, LANES), F32),
            dma((PARTS, 2)),
            dma((PARTS + 1, 2)),
        ],
        compiler_params=pltpu.CompilerParams(vmem_limit_bytes=62 << 20),
    )(*middle)


def solution(mesh):
    body = functools.partial(per_device, n_mesh=mesh.shape["mesh"], n_samp=mesh.shape["samp"])
    return jax.shard_map(
        body,
        mesh=mesh,
        in_specs=(
            P("samp", "mesh"),
            P("samp", "mesh"),
            P("samp", "mesh"),
            P("mesh", None, None),
            P("mesh"),
            P("mesh", None),
            P("mesh", None),
            P("mesh"),
        ),
        out_specs=(P("samp", "mesh"), P("samp", "mesh"), P(None, "samp")),
        check_vma=False,
    )
```

```python
import functools

import jax
import jax.numpy as jnp
from jax import lax
from jax.experimental import pallas as pl
from jax.experimental.pallas import tpu as pltpu
from jax.sharding import PartitionSpec as P

MESH = pl.DeviceIdType.MESH
F32 = jnp.float32
BF16 = jnp.bfloat16
LANES = 128
BLK = 192
PAIR = 2 * BLK
SLOTS = 6
GHOST = 8
ITERS = 2
TILES = 4
REACH = 4
SQUARE = 4
PARTS = 2


def nt(a, b):
    return lax.dot_general(a, b, (((1,), (1,)), ((), ())), preferred_element_type=F32)


def nn(a, b):
    return lax.dot_general(a, b, (((1,), (0,)), ((), ())), preferred_element_type=F32)


def split2(x):
    high = x.astype(BF16).astype(F32)
    return jnp.concatenate([high, x - high], 1).astype(BF16)


def halves(x):
    rows = x.shape[0] // 2
    return x[:rows] + x[rows:]


def turned(x):
    return pltpu.roll(x, LANES // 2, 1)


def kernel(
    n_mesh, n_samp,
    resid, u_in, c_in, stiff, diag, pattern_in, send_in, sizes_in,
    fields_out, panels_out, fin_out, coef_out,
    r, a, b, r_next, w_next, base_sol, fin, coef_t, own,
    uc_loc, st, dg, pattern, send_list, sizes,
    stage, panel_send, panel_got, spread, cn, un, dn, rb, wb,
    t0, t1, r0t, send_f, got_f, send_c, got_c,
    pay, rs_got, ar_got,
    in_sems, panel_ssem, panel_rsem, ghost_ssem, ghost_rsem, rs_ssem, rs_rsem, ag_ssem, ag_rsem, out_sems, far_sem,
):
    me = lax.axis_index("mesh")
    mine = lax.axis_index("samp")
    cols, dofs = r.shape
    recy = cn.shape[0] // 2
    rows_per = recy // n_samp
    quarters = 16 // rows_per
    wide = dofs // quarters // LANES
    pairs = dofs // PAIR
    low_half = lax.broadcasted_iota(jnp.int32, (cols, LANES), 1) < LANES // 2

    loads = [
        pltpu.make_async_copy(src, dst, in_sems.at[i])
        for i, (src, dst) in enumerate(
            (
                (c_in, uc_loc.at[0]),
                (sizes_in, sizes),
                (resid, r),
                (send_in, send_list),
                (u_in, uc_loc.at[1]),
                (diag, dg),
                (pattern_in, pattern),
                (stiff, st),
            )
        )
    ]
    for load in loads:
        load.start()

    barrier = pltpu.get_barrier_semaphore()
    chips = n_mesh // 2
    chip, core = lax.div(me, 2), lax.rem(me, 2)

    side = SQUARE
    row, column = lax.div(mine, side), lax.rem(mine, side)
    ring = [min(k, side - k) for k in range(side)]
    hops = sorted(range(1, n_samp), key=lambda o: -(ring[o // side] + ring[o % side]))
    peers = [side * lax.rem(row + o // side, side) + lax.rem(column + o % side, side) for o in hops]

    def greet(**device):
        pl.semaphore_signal(barrier, inc=1, device_id=device, device_id_type=MESH)

    for away in range(REACH, 0, -1):
        for by in (away, chips - away):
            for which in range(2):
                greet(mesh=2 * lax.rem(chip + by, chips) + which)
        if away == REACH:
            for peer in peers:
                greet(samp=peer)
    greet(mesh=2 * chip + 1 - core)

    def row_alive(start, width):
        live = sizes[0] * BLK
        return (lax.broadcasted_iota(jnp.int32, (1, width), 1) + start) < live

    def pack_panel(which):
        local = uc_loc[which].astype(F32)
        for q in range(quarters):
            for t in range(wide):
                at = (q * wide + t) * LANES
                stage[which, t, pl.ds(q, rows_per, stride=quarters), :] = local[:, at : at + LANES]
        packed = stage[which].astype(BF16)
        panel_send[which] = packed
        panel_got[which, mine] = packed

    def send_panel(which):
        for peer in peers:
            pltpu.make_async_remote_copy(
                src_ref=panel_send.at[which],
                dst_ref=panel_got.at[which, mine],
                send_sem=panel_ssem.at[which],
                recv_sem=panel_rsem.at[which],
                device_id={"samp": peer},
                device_id_type=MESH,
            ).start()

    def wait_panel(which, sems):
        others = panel_got.at[which, pl.ds(0, n_samp - 1)]
        pltpu.make_async_copy(others, others, sems.at[which]).wait()

    def natural(which, out):
        for k in range(n_samp):
            for t in range(wide):
                spread[t, 16 * k : 16 * k + 16, :] = panel_got[which, k, t].astype(F32)
        for q in range(quarters):
            for t in range(wide):
                at = (q * wide + t) * LANES
                tile = spread[t, pl.ds(q, recy, stride=quarters), :]
                tile = jnp.where(row_alive(at, LANES), tile, 0.0).astype(BF16)
                out[:recy, at : at + LANES] = tile
                out[recy:, at : at + LANES] = tile

    span = chips // 2
    back = span // 2 - 1
    part = lax.rem(chip, span)
    reducer = jnp.logical_and(core == lax.rem(part, 2), part < TILES)
    own_sum = lax.div(chip, span) * TILES + part
    all_sums = 2 * TILES

    rows_packed = cols // 2 // TILES
    eye = lax.broadcasted_iota(jnp.int32, (cols, cols), 0) == lax.broadcasted_iota(jnp.int32, (cols, cols), 1)

    def as_row(column):
        return jnp.sum(jnp.where(eye, column, 0.0), axis=0, keepdims=True)

    def as_column(row):
        return jnp.sum(jnp.where(eye, row, 0.0), axis=1, keepdims=True)

    def rs_send(which, value, extra):
        packed = jnp.concatenate([value[: cols // 2], value[cols // 2 :]], 1)
        for t in range(TILES):
            pay[which, t, :rows_packed] = packed[rows_packed * t : rows_packed * (t + 1), :]
            pay[which, t, rows_packed:] = extra

        for t in range(TILES):
            away = lax.rem(chip - t + chips + back, chips)
            slot = 2 * lax.rem(away, span) + core
            target = 2 * lax.rem(t + span * lax.div(away, span), chips) + t % 2

            @pl.when(target != me)
            def _(t=t, slot=slot, target=target):
                pltpu.make_async_remote_copy(
                    src_ref=pay.at[which, t],
                    dst_ref=rs_got.at[which, slot],
                    send_sem=rs_ssem.at[which],
                    recv_sem=rs_rsem.at[which],
                    device_id={"mesh": target},
                    device_id_type=MESH,
                ).start()

            @pl.when(target == me)
            def _(t=t, slot=slot):
                rs_got[which, slot] = pay[which, t]

    def tiles_done(sem, count):
        some = ar_got.at[pl.ds(0, count)]
        pltpu.make_async_copy(some, some, sem).wait()

    def ag_send(which):
        @pl.when(reducer)
        def _():
            tiles_done(rs_rsem.at[which], 2 * span - 1)
            total = rs_got[which, 0]
            for d in range(1, 2 * span):
                total = total + rs_got[which, d]
            at = which * all_sums + own_sum
            ar_got[at] = total

            half = n_mesh // 2
            for ahead in sorted(range(1, n_mesh), key=lambda k: abs(k - half)):
                pltpu.make_async_remote_copy(
                    src_ref=ar_got.at[at],
                    dst_ref=ar_got.at[at],
                    send_sem=ag_ssem.at[which],
                    recv_sem=ag_rsem.at[which],
                    device_id={"mesh": lax.rem(me + ahead, n_mesh)},
                    device_id_type=MESH,
                ).start()

    def ar_wait(which):
        @pl.when(reducer)
        def _():
            tiles_done(ag_rsem.at[which], all_sums - 1)

        @pl.when(jnp.logical_not(reducer))
        def _():
            tiles_done(ag_rsem.at[which], all_sums)

        at = which * all_sums
        tiles = [ar_got[at + t] + ar_got[at + TILES + t] for t in range(TILES)]
        packed = jnp.concatenate([tile[:rows_packed] for tile in tiles], 0)
        value = jnp.concatenate([packed[:, :recy], packed[:, recy:]], 0)
        return value, tiles[0][rows_packed:]

    def ar_sent(which):
        @pl.when(reducer)
        def _():
            tiles_done(rs_ssem.at[which], TILES - 1)
            tiles_done(ag_ssem.at[which], n_mesh - 1)

        @pl.when(jnp.logical_not(reducer))
        def _():
            tiles_done(rs_ssem.at[which], TILES)

    def fill_tables(m, row, tiles):
        n0, n1, n2 = tiles
        b0, b1, b2 = n0.astype(BF16), n1.astype(BF16), n2.astype(BF16)
        v0, v1, v2 = turned(n0).astype(BF16), turned(n1).astype(BF16), turned(n2).astype(BF16)
        even, odd, rows = 2 * m, 2 * m + 1, slice(row, row + cols)
        t0[even, rows] = b0
        r0t[even, rows] = v0
        t1[even, rows] = jnp.where(low_half, b1, v1)
        t0[odd, rows] = jnp.where(low_half, v1, v2)
        r0t[odd, rows] = jnp.where(low_half, b2, b1)
        t1[odd, rows] = jnp.where(low_half, v2, b2)

    def fill_split(source):
        def one(m, carry):
            at = pl.multiple_of(m * PAIR, PAIR)
            tiles = [source[:, pl.ds(at + j * LANES, LANES)] for j in range(3)]
            fill_tables(m, 0, tiles)
            fill_tables(m, cols, [x - x.astype(BF16).astype(F32) for x in tiles])
            return carry

        lax.fori_loop(0, pairs, one, 0, unroll=2)

    def ghost_copies(send, got, which):
        out = []
        for side, by in ((0, 1), (1, n_mesh - 1)):
            out.append(
                pltpu.make_async_remote_copy(
                    src_ref=send.at[side],
                    dst_ref=got.at[side],
                    send_sem=ghost_ssem.at[which, side],
                    recv_sem=ghost_rsem.at[which, side],
                    device_id={"mesh": lax.rem(me + by, n_mesh)},
                    device_id_type=MESH,
                )
            )
        return out

    def pack_ghosts(send, row, rows, copies=()):
        ends = (me == n_mesh - 1, me == 0)
        for side in range(2):
            keep = jnp.where(ends[side], 0.0, 1.0).astype(BF16)
            for start in range(0, rows, cols):
                span, to = slice(row + start, row + start + cols), slice(start, start + cols)
                for pair in range(GHOST // 2):
                    x, y = send_list[side, 2 * pair], send_list[side, 2 * pair + 1]
                    send[side, 2 * pair, to] = t0[x, span] * keep
                    send[side, 2 * pair + 1, to] = t0[y, span] * keep
                    send[side, GHOST + pair, to] = jnp.where(low_half, t1[x, span], t1[y, span]) * keep
            if copies:
                copies[side].start()

    def take_ghosts(got, row, rows):
        for side in range(2):
            base = 2 * pairs + side * GHOST
            for start in range(0, rows, cols):
                span, to = slice(start, start + cols), slice(row + start, row + start + cols)
                for pair in range(GHOST // 2):
                    for j in range(2):
                        x = got[side, 2 * pair + j, span]
                        t0[base + 2 * pair + j, to] = x
                        r0t[base + 2 * pair + j, to] = turned(x.astype(F32)).astype(BF16)
                    x = got[side, GHOST + pair, span]
                    y = turned(x.astype(F32)).astype(BF16)
                    t1[base + 2 * pair, to] = jnp.where(low_half, x, y)
                    t1[base + 2 * pair + 1, to] = jnp.where(low_half, y, x)

    def by_pairs(rows, low_rows, lanes, left, emit):
        def one(m, carry):
            at = pl.multiple_of(m * PAIR, PAIR)
            out0 = nt(left(2 * m), st[pl.ds(at, 2 * LANES), lanes])
            out1 = nt(left(2 * m + 1), st[pl.ds(at + LANES, 2 * LANES), lanes])
            emit(at, 0, out0[:, :LANES])
            emit(at, 1, jnp.where(low_rows, out0[:, LANES:], out1[:, :LANES]))
            emit(at, 2, out1[:, LANES:])
            return carry

        lax.fori_loop(0, pairs, one, 0, unroll=4)

    def apply_own(rows):
        low_rows = lax.broadcasted_iota(jnp.int32, (rows, LANES), 1) < LANES // 2
        none = jnp.zeros((rows, LANES), BF16)

        def left(i):
            return jnp.concatenate([t0[i, :rows], jnp.where(low_rows, t1[i, :rows], none)], 1)

        def emit(at, j, value):
            own[:rows, pl.ds(at + j * LANES, LANES)] = value

        by_pairs(rows, low_rows, slice(0, 2 * LANES), left, emit)

    def apply_stiff(rows, emit):
        low_rows = lax.broadcasted_iota(jnp.int32, (rows, LANES), 1) < LANES // 2
        none = jnp.zeros((rows, LANES), BF16)

        def left(i):
            parts = []
            for s in range(0, SLOTS, 2):
                x, y = pattern[s, i], pattern[s + 1, i]
                turned_y = r0t[y, :rows]
                if s:
                    parts.append(t0[x, :rows])
                parts.append(jnp.where(low_rows, t1[x, :rows] if s else none, turned_y))
                parts.append(jnp.where(low_rows, turned_y, t1[y, :rows]))
            return jnp.concatenate(parts, 1)

        def whole(at, j, value):
            emit(at, j, value + own[:rows, pl.ds(at + j * LANES, LANES)])

        by_pairs(rows, low_rows, slice(LANES, SLOTS * BLK), left, whole)

    def emit_first(at, j, value):
        span = pl.ds(at + j * LANES, LANES)
        keep, scale = row_alive(at + j * LANES, LANES), dg[:, span]
        a[:, span] = jnp.where(keep, halves(value[: 2 * cols]) + scale * r[:, span], 0.0)
        image = value[2 * cols :] + scale * cn[:recy, span].astype(F32)
        image = jnp.where(keep, image, 0.0).astype(BF16)
        dn[:recy, span] = image
        dn[recy:, span] = image

    def emit_second(at, j, value):
        span = pl.ds(at + j * LANES, LANES)
        b[:, span] = jnp.where(
            row_alive(at + j * LANES, LANES), halves(value) + dg[:, span] * a[:, span], 0.0
        )

    def renew(make, r_to, w_to):
        def one(m, carry):
            ww, wr = carry
            at = pl.multiple_of(m * PAIR, PAIR)
            span = pl.ds(at, PAIR)
            new_r, image = make(span)
            r_to[:, span] = new_r
            w_to[:, span] = image
            high = image.astype(BF16)
            wb[:cols, span] = high
            wb[cols:, span] = (image - high.astype(F32)).astype(BF16)
            for j in range(3):
                x = image[:, j * LANES : (j + 1) * LANES]
                ww = ww + x * x
                wr = wr + x * new_r[:, j * LANES : (j + 1) * LANES]
            return ww, wr

        zero = jnp.zeros((cols, LANES), F32)
        ww, wr = lax.fori_loop(0, pairs, one, (zero, zero), unroll=4)
        proj = halves(nt(wb[...], cn[:recy]))
        ww = jnp.sum(ww, axis=1, keepdims=True)
        wr = jnp.sum(wr, axis=1, keepdims=True)
        return proj, jnp.concatenate([as_row(ww), as_row(wr)], 1)

    def times_gram(x):
        high = x.astype(BF16).astype(F32)
        gram_high = gram.astype(BF16).astype(F32)
        left = jnp.concatenate([high, x - high, high], 1).astype(BF16)
        return nn(left, jnp.concatenate([gram_high, gram_high, gram - gram_high], 0).astype(BF16))

    def step_of(reduced, c_r):
        proj, extra = reduced
        ww, wr = as_column(extra[:, :cols]), as_column(extra[:, cols:])
        p_gram = times_gram(proj)
        bottom = ww + jnp.sum(proj * (p_gram - 2.0 * proj), axis=1, keepdims=True)
        top = wr - jnp.sum(proj * c_r, axis=1, keepdims=True)
        step = top / bottom
        return proj, step, c_r - step * (proj - p_gram)

    loads[0].wait()
    pack_panel(0)
    pl.semaphore_wait(barrier, 4 * REACH + n_samp)
    for by in (REACH, chips - REACH):
        peer = 2 * lax.rem(chip + by, chips) + core
        pl.semaphore_signal(far_sem, inc=1, device_id={"mesh": peer}, device_id_type=MESH)
    send_panel(0)
    loads[1].wait()
    loads[2].wait()

    def mask(m, carry):
        at = pl.multiple_of(m * PAIR, PAIR)
        span = pl.ds(at, PAIR)
        kept = jnp.where(row_alive(at, PAIR), r[:, span], 0.0)
        r[:, span] = kept
        rb[:, span] = kept.astype(BF16)
        return carry

    lax.fori_loop(0, pairs, mask, 0)
    fill_split(r)
    loads[3].wait()
    pack_ghosts(send_f.at[0], 0, 2 * cols, ghost_copies(send_f.at[0], got_f.at[0], 0))
    loads[4].wait()
    pack_panel(1)
    wait_panel(0, panel_rsem)
    natural(0, cn)
    first = nt(jnp.concatenate([rb[...], cn[:recy]], 0), cn[:recy])
    no_extra = jnp.zeros((1, LANES), F32)
    rs_send(0, first[:cols], no_extra)
    rs_send(ITERS + 1, first[cols:], no_extra)

    def fill_panel(m, carry):
        at = pl.multiple_of(m * PAIR, PAIR)
        fill_tables(m, 2 * cols, [cn[:recy, pl.ds(at + j * LANES, LANES)].astype(F32) for j in range(3)])
        return carry

    lax.fori_loop(0, pairs, fill_panel, 0, unroll=2)
    pack_ghosts(send_c, 2 * cols, recy, ghost_copies(send_c, got_c, 1))
    for copy in ghost_copies(send_f.at[0], got_f.at[0], 0):
        copy.wait()
    take_ghosts(got_f.at[0], 0, 2 * cols)
    for load in loads[5:]:
        load.wait()
    apply_own(2 * cols + recy)
    pl.semaphore_wait(far_sem, 2)
    ag_send(0)
    for copy in ghost_copies(send_c, got_c, 1):
        copy.wait()
    take_ghosts(got_c, 2 * cols, recy)
    apply_stiff(2 * cols + recy, emit_first)
    coef, _ = ar_wait(0)
    coef2 = split2(coef)

    def make_first(span):
        new_r = r[:, span] - nn(coef2, cn[:, span])
        return new_r, a[:, span] - nn(coef2, dn[:, span])

    rs_send(1, *renew(make_first, r, a))

    coef_t[...] = coef.T
    fill_split(a)
    pack_ghosts(send_f.at[1], 0, 2 * cols, ghost_copies(send_f.at[1], got_f.at[1], 2))
    ag_send(ITERS + 1)
    apply_own(2 * cols)
    ag_send(1)
    send_panel(1)
    for copy in ghost_copies(send_f.at[1], got_f.at[1], 2):
        copy.wait()
    take_ghosts(got_f.at[1], 0, 2 * cols)
    apply_stiff(2 * cols, emit_second)
    gram, _ = ar_wait(ITERS + 1)
    c_r = coef - times_gram(coef)
    proj, step1, c_r = step_of(ar_wait(1), c_r)
    proj2 = split2(proj)

    def make_second(span):
        image = a[:, span]
        new_r = r[:, span] - step1 * (image - nn(proj2, cn[:, span]))
        return new_r, image - step1 * (b[:, span] - nn(proj2, dn[:, span]))

    rs_send(2, *renew(make_second, r_next, w_next))

    wait_panel(1, panel_rsem)
    natural(1, un)
    carried2 = split2(coef - step1 * proj)

    def base(m, carry):
        span = pl.ds(pl.multiple_of(m * PAIR, PAIR), PAIR)
        rounded = r[:, span].astype(BF16).astype(F32)
        base_sol[:, span] = nn(carried2, un[:, span]) + step1 * rounded
        return carry

    lax.fori_loop(0, pairs, base, 0, unroll=2)
    outs = [
        pltpu.make_async_copy(src, dst, out_sems.at[i])
        for i, (src, dst) in enumerate(
            (
                (r_next, fields_out.at[0]),
                (w_next, fields_out.at[1]),
                (base_sol, fields_out.at[2]),
                (cn.at[:recy], panels_out.at[0]),
                (un.at[:recy], panels_out.at[1]),
                (coef_t, coef_out),
                (fin, fin_out),
            )
        )
    ]
    for copy in outs[:6]:
        copy.start()
    for which in range(2):
        wait_panel(which, panel_ssem)
        ar_sent(which)
    ar_sent(ITERS + 1)
    ag_send(2)
    proj, step2, _ = step_of(ar_wait(2), c_r)
    fin[...] = jnp.concatenate([proj, jnp.broadcast_to(step2, (cols, LANES - recy))], 1)
    outs[6].start()
    ar_sent(2)
    for copy in outs:
        copy.wait()

def last_kernel(
    fields_in, panels_in, fin_in, coef_in,
    sol_out, res_out, coef_out,
    fields, panels, fin, in_sems, out_sems,
):
    _, cols, dofs = fields.shape
    recy = panels.shape[1]
    width = dofs // PARTS
    fin_copy = pltpu.make_async_copy(fin_in, fin, out_sems.at[0, 1])
    fin_copy.start()
    loads, outs = [], []
    for i in range(PARTS):
        span = pl.ds(i * width, width)
        loads.append(
            [
                pltpu.make_async_copy(src.at[:, :, span], dst.at[:, :, span], in_sems.at[i, j])
                for j, (src, dst) in enumerate(((panels_in, panels), (fields_in, fields)))
            ]
        )
        for load in loads[-1]:
            load.start()
    coef_copy = pltpu.make_async_copy(coef_in, coef_out, out_sems.at[0, 0])
    coef_copy.start()
    fin_copy.wait()
    proj, step = fin[:, :recy], fin[:, recy : recy + 1]
    high = proj.astype(BF16)
    proj2 = jnp.concatenate([high, (proj - high.astype(F32)).astype(BF16)], 0)
    for i in range(PARTS):
        for load in loads[i]:
            load.wait()
        at = slice(i * width, (i + 1) * width)
        old = fields[0, :, at]
        fields[0, :, at] = old - step * (fields[1, :, at] - halves(nn(proj2, panels[0, :, at])))
        rounded = old.astype(BF16).astype(F32)
        fields[2, :, at] = fields[2, :, at] + step * (rounded - halves(nn(proj2, panels[1, :, at])))
        for j, dst in ((0, res_out), (2, sol_out)):
            span = pl.ds(i * width, width)
            out = pltpu.make_async_copy(fields.at[j, :, span], dst.at[:, span], out_sems.at[i + 1, j // 2])
            out.start()
            outs.append(out)
    coef_copy.wait()
    for out in outs:
        out.wait()


def per_device(resid_in, recycle_u, recycle_c, stiff, diag_scale, pattern, send_list, part_sizes, n_mesh, n_samp):
    cols, dofs = resid_in.shape
    blocks, blk, width = stiff.shape
    recy = recycle_c.shape[0] * n_samp
    wide = dofs * recycle_c.shape[0] // 16 // LANES
    ext = blocks + 2 * GHOST
    tile = cols // 2 // TILES + 1
    hbm = pl.BlockSpec(memory_space=pltpu.HBM)
    dma = pltpu.SemaphoreType.DMA
    field = pltpu.VMEM((cols, dofs), F32)
    panel = pltpu.VMEM((2 * recy, dofs), BF16)
    table = pltpu.VMEM((ext, 2 * cols + recy, LANES), BF16)
    middle = pl.pallas_call(
        functools.partial(kernel, n_mesh, n_samp),
        out_shape=(
            jax.ShapeDtypeStruct((3, cols, dofs), F32),
            jax.ShapeDtypeStruct((2, recy, dofs), BF16),
            jax.ShapeDtypeStruct((cols, LANES), F32),
            jax.ShapeDtypeStruct((recy, cols), F32),
        ),
        in_specs=[hbm] * 8,
        out_specs=(hbm,) * 4,
        scratch_shapes=[
            field,
            field,
            field,
            field,
            field,
            field,
            pltpu.VMEM((cols, LANES), F32),
            pltpu.VMEM((recy, cols), F32),
            pltpu.VMEM((2 * cols + recy, dofs), F32),
            pltpu.VMEM((2, recycle_c.shape[0], dofs), BF16),
            pltpu.VMEM((blocks * blk, width), BF16),
            pltpu.VMEM((1, dofs), F32),
            pltpu.SMEM(pattern.shape[::-1], jnp.int32),
            pltpu.SMEM(send_list.shape, jnp.int32),
            pltpu.SMEM(part_sizes.shape, jnp.int32),
            pltpu.VMEM((2, wide, 16, LANES), F32),
            pltpu.VMEM((2, wide, 16, LANES), BF16),
            pltpu.VMEM((2, n_samp, wide, 16, LANES), BF16),
            pltpu.VMEM((wide, 16 * n_samp, LANES), F32),
            panel,
            panel,
            panel,
            pltpu.VMEM((cols, dofs), BF16),
            pltpu.VMEM((2 * cols, dofs), BF16),
            table,
            table,
            table,
            pltpu.VMEM((ITERS, 2, GHOST + GHOST // 2, 2 * cols, LANES), BF16),
            pltpu.VMEM((ITERS, 2, GHOST + GHOST // 2, 2 * cols, LANES), BF16),
            pltpu.VMEM((2, GHOST + GHOST // 2, recy, LANES), BF16),
            pltpu.VMEM((2, GHOST + GHOST // 2, recy, LANES), BF16),
            pltpu.VMEM((ITERS + 2, TILES, tile, LANES), F32),
            pltpu.VMEM((ITERS + 2, n_mesh // 2, tile, LANES), F32),
            pltpu.VMEM(((ITERS + 2) * 2 * TILES, tile, LANES), F32),
            dma((8,)),
            dma((2,)),
            dma((2,)),
            dma((ITERS + 1, 2)),
            dma((ITERS + 1, 2)),
            dma((ITERS + 2,)),
            dma((ITERS + 2,)),
            dma((ITERS + 2,)),
            dma((ITERS + 2,)),
            dma((7,)),
            pltpu.SemaphoreType.REGULAR,
        ],
        compiler_params=pltpu.CompilerParams(
            collective_id=0, has_side_effects=True, vmem_limit_bytes=62 << 20
        ),
    )(
        resid_in,
        recycle_u,
        recycle_c,
        stiff.reshape(blocks * blk, width),
        diag_scale.reshape(1, dofs),
        pattern.T,
        send_list,
        part_sizes,
    )
    return pl.pallas_call(
        last_kernel,
        out_shape=(
            jax.ShapeDtypeStruct((cols, dofs), F32),
            jax.ShapeDtypeStruct((cols, dofs), F32),
            jax.ShapeDtypeStruct((recy, cols), F32),
        ),
        in_specs=[hbm] * 4,
        out_specs=(hbm,) * 3,
        scratch_shapes=[
            pltpu.VMEM((3, cols, dofs), F32),
            pltpu.VMEM((2, recy, dofs), BF16),
            pltpu.VMEM((cols, LANES), F32),
            dma((PARTS, 2)),
            dma((PARTS + 1, 2)),
        ],
        compiler_params=pltpu.CompilerParams(vmem_limit_bytes=62 << 20),
    )(*middle)


def solution(mesh):
    body = functools.partial(per_device, n_mesh=mesh.shape["mesh"], n_samp=mesh.shape["samp"])
    return jax.shard_map(
        body,
        mesh=mesh,
        in_specs=(
            P("samp", "mesh"),
            P("samp", "mesh"),
            P("samp", "mesh"),
            P("mesh", None, None),
            P("mesh"),
            P("mesh", None),
            P("mesh", None),
            P("mesh"),
        ),
        out_specs=(P("samp", "mesh"), P("samp", "mesh"), P(None, "samp")),
        check_vma=False,
    )
```
